256 devices in a mesh: row: 32 (over z, x_lo, core), col: 8 (over y, x_hi).
Axes of the slice: x: 4 (x_hi: 2, x_lo: 2; x = x_hi * 2 + x_lo), y: 4, z: 8, core: 2. Of those that a mesh axis runs over, the one named last changes fastest.
Arguments:
- activations: bfloat16 [512, 8192], P('col', 'row'), may hold values from -6 to 6
- cotangent: bfloat16 [512, 14336], P('row', 'col'), may hold values from -0.109375 to 0.109375
- accumulated: bfloat16 [8192, 14336], P('row', 'col'), may hold values from -3 to 3
- band_old: float32 [8192, 16, 256], P('row', 'col'), may hold values from -6 to 6
- diagonal_old: float32 [8192, 256], P(('row', 'col')), may hold values from -6 to 6
Outputs:
- band_new: float32 [8192, 16, 256], P('row', 'col')
- diagonal_new: float32 [8192, 256], P(('row', 'col'))
The draws below stay inside these ranges and needn't reach their ends.
All inputs are finite; a program needn't handle non-finite values.
Results may differ from the reference program's by a relative error of at most 0.0018.
Values may be sent and summed in bfloat16 or wider, within the bound.
A program may use at most 64 MiB of HBM per device.

```python
import jax
import jax.numpy as jnp
from jax import lax

D = 8192
FF = 14336
TOKENS = 512
BLOCK = 256
BAND = 16
N_ROW = 32


def shard_levels(key, dims, shards, smallest, largest):
    gain = 1.0
    for position, parts in shards:
        draws = jax.random.uniform(jax.random.fold_in(jax.random.fold_in(key, 6), position), (parts,), jnp.float32, smallest / len(shards), largest / len(shards))
        gain = gain * jnp.repeat(jnp.exp(draws), dims[position] // parts).reshape((-1,) + (1,) * (len(dims) - 1 - position))
    return gain


def gaussian(key, dims, width, most, shards=(), kind=jnp.bfloat16):
    loudness = shard_levels(key, dims, shards, -0.22, 0.18) if shards else 1.0
    values = jax.random.normal(key, dims, jnp.float32) * width * loudness
    return jnp.minimum(jnp.maximum(values, -most), most).astype(kind)


def setup_inputs(seed: int = 0) -> dict:
    splits = jax.random.split(jax.random.key(seed), 6)
    activations = gaussian(splits[0], (TOKENS, D), 1.0, 6.0, ((0, 8), (1, 32)))
    cotangent = gaussian(splits[1], (TOKENS, FF), (6 * TOKENS) ** -0.5, 0.109375, ((0, 32), (1, 8)))
    accumulated = gaussian(splits[2], (D, FF), 0.5, 3.0, ((0, 32), (1, 8)))
    band_old = gaussian(splits[3], (D, BAND, BLOCK), 1.0, 6.0, ((0, 32), (1, 8)), jnp.float32)
    diagonal_old = gaussian(splits[4], (D, BLOCK), 1.0, 6.0, ((0, 256),), jnp.float32)
    return {"activations": activations, "cotangent": cotangent, "accumulated": accumulated, "band_old": band_old, "diagonal_old": diagonal_old}


decay_rate = 0.95


def reference(activations, cotangent, accumulated, band_old, diagonal_old):
    product = jnp.dot(activations.T, cotangent, preferred_element_type=jnp.float32)
    gradient = (product + accumulated.astype(jnp.float32)).astype(jnp.bfloat16)
    blocks = gradient.astype(jnp.float32).reshape(N_ROW, D // N_ROW, FF)
    self_gram = jnp.einsum("rak,rbk->rab", blocks, blocks, precision=lax.Precision.HIGHEST)
    band_list = []
    for offset in range(1, N_ROW // 2 + 1):
        shifted = jnp.roll(blocks, offset, axis=0)
        band_list.append(jnp.einsum("rak,rbk->rab", blocks, shifted, precision=lax.Precision.HIGHEST))
    stacked = jnp.stack(band_list, axis=2).reshape(D, N_ROW // 2, D // N_ROW)
    band_new = decay_rate * band_old + (1.0 - decay_rate) * stacked
    diagonal_new = decay_rate * diagonal_old + (1.0 - decay_rate) * self_gram.reshape(D, D // N_ROW)
    return (band_new, diagonal_new)
```

```python
import jax
import jax.numpy as jnp
from jax import lax
from jax.experimental import pallas as pl
from jax.experimental.pallas import tpu as pltpu
from jax.sharding import PartitionSpec as P

MESH = pl.DeviceIdType.MESH
DECAY = 0.95
CHUNKS = 4

A0, AM1, AP1, AM2, AP2, XP, XM, XX, STAGE = range(9)
PLACE = {A0: (0, 0), AM1: (-1, 0), AP1: (1, 0), AM2: (-2, 0), AP2: (2, 0), XP: (2, 1), XM: (2, -1), XX: (2, 2)}
TASKS = (
    (A0, A0),
    (A0, AM1), (AP1, AM1),
    (AP1, AM2), (AP2, AM2),
    (XP, AP2), (XP, AP1), (XP, A0), (XP, AM1), (XP, AM2), (XM, AP1), (XM, A0), (XM, AM1),
    (XX, AP1), (XX, A0), (XX, AM1), (XX, None),
)
PHASES = (0, 1, 3, 5, 13, 17)
N = len(TASKS)


def pick(index, values):
    result = jnp.int32(values[0])
    for i, value in enumerate(values):
        if i and value != values[0]:
            result = jnp.where(index == i, jnp.int32(value), result)
    return result


def kernel(
    act_ref, cot_ref, acc_ref, band_ref, diag_ref, band_out, diag_out,
    act_all, cot_all, pan, prod, core_in, half, y_in, piece, fin, fin_diag,
    act_s, act_r, cz_s, cz_r, cx_s, cx_r, cc_s, cc_r, sw_s, sw_r, pan_s, pan_r,
    core_s, core_r, y_s, y_r, fin_s, fin_r, find_r,
):
    row = lax.axis_index("row")
    col = lax.axis_index("col")
    z, xl, co = row // 4, lax.rem(row // 2, 2), lax.rem(row, 2)
    y, xh = col // 2, lax.rem(col, 2)
    x = 2 * xh + xl

    def at(row_, col_):
        return {"row": row_, "col": col_}

    def dev(dz, dx, dy, core):
        zz, xx, yy = lax.rem(z + dz + 8, 8), lax.rem(x + dx + 4, 4), lax.rem(y + dy + 4, 4)
        return at(4 * zz + 2 * lax.rem(xx, 2) + core, 2 * yy + xx // 2)

    def send(src, dst, s_sem, r_sem, device):
        return pltpu.make_async_remote_copy(
            src_ref=src, dst_ref=dst, send_sem=s_sem, recv_sem=r_sem, device_id=device, device_id_type=MESH
        )

    def arrived(dst, sem):
        pltpu.make_async_copy(dst, dst, sem).wait()

    sent = []

    def start(*args):
        copy = send(*args)
        copy.start()
        sent.append(copy)

    z_peers = [at(lax.rem(row + 4 * k, 32), col) for k in range(1, 8)]
    col_peers = [at(row, lax.rem(col + k, 8)) for k in range(1, 8)]
    core_row = row + 1 - 2 * co
    xl_row = row + 2 - 4 * xl
    other_col = col + 1 - 2 * xh
    barrier = pltpu.get_barrier_semaphore()
    greet = z_peers + col_peers + [at(core_row, col), at(xl_row, col), at(xl_row, other_col), at(core_row, other_col)]
    for peer in greet:
        pl.semaphore_signal(barrier, inc=1, device_id=peer, device_id_type=MESH)
    pl.semaphore_wait(barrier, len(greet))

    def cot_piece(row_):
        return cot_all.at[pl.ds(pl.multiple_of(16 * row_, 16), 16)]

    def act_piece(col_):
        return act_all.at[pl.ds(pl.multiple_of(64 * col_, 64), 64)]

    order = (1, 7, 2, 6, 3, 5, 4)
    for k in order:
        start(cot_ref, cot_piece(row), cz_s.at[k], cz_r.at[k], at(lax.rem(row + 4 * k, 32), col))
    start(cot_ref, cot_piece(row), cx_s.at[0], cx_r.at[0], at(xl_row, col))
    start(cot_ref, cot_piece(row), cc_s.at[0], cc_r.at[0], at(core_row, col))
    for k in range(1, 8):
        start(act_ref, act_piece(col), act_s.at[k], act_r.at[k], at(row, lax.rem(col + k, 8)))
    cot_piece(row)[...] = cot_ref[...]
    act_piece(col)[...] = act_ref[...]
    for k in order:
        source = lax.rem(row - 4 * k + 32, 32)
        arrived(cot_piece(source), cz_r.at[k])
        start(cot_piece(source), cot_piece(source), cx_s.at[k], cx_r.at[k], at(xl_row, col))
        start(cot_piece(source), cot_piece(source), cc_s.at[k], cc_r.at[k], at(core_row, col))
    for k in (0,) + order:
        source = lax.rem(xl_row - 4 * k + 32, 32)
        arrived(cot_piece(source), cx_r.at[k])
        start(cot_piece(source), cot_piece(source), cc_s.at[8 + k], cc_r.at[8 + k], at(core_row, col))
    for k in range(1, 8):
        source = lax.rem(col - k + 8, 8)
        arrived(act_piece(source), act_r.at[k])
    for k in (0,) + order:
        source = lax.rem(core_row - 4 * k + 32, 32)
        arrived(cot_piece(source), cc_r.at[k])
    for k in (0,) + order:
        source = lax.rem(core_row + 2 - 4 * xl - 4 * k + 32, 32)
        arrived(cot_piece(source), cc_r.at[8 + k])

    same = xh == co
    own = jnp.where(same, A0, STAGE)
    size = 256 // CHUNKS

    def chunk(slot, i):
        return pan.at[slot, pl.ds(size * i, size)]

    def swap(i):
        return send(chunk(STAGE, i), chunk(A0, i), sw_s.at[i], sw_r.at[i], at(4 * z + 2 * xl + xh, 2 * y + co))

    tall = 128
    for j in range(256 // tall):
        left = act_all[:, tall * j : tall * (j + 1)].T
        rows = pl.ds(tall * j, tall)

        @pl.loop(0, 7)
        def _(n):
            columns = pl.ds(pl.multiple_of(256 * n, 256), 256)
            product = jnp.dot(left, cot_all[:, columns], preferred_element_type=jnp.float32)
            pan[own, rows, columns] = (product + acc_ref[rows, columns].astype(jnp.float32)).astype(jnp.bfloat16)

        per = CHUNKS * tall // 256

        @pl.when(jnp.logical_not(same))
        def _():
            for i in range(per * j, per * (j + 1)):
                swap(i).start()

    def over_z(i, source, up, down):
        start(chunk(source[0], i), chunk(up, i), pan_s.at[up, i], pan_r.at[up, i], dev(1, 0, 0, co))
        start(chunk(source[1], i), chunk(down, i), pan_s.at[down, i], pan_r.at[down, i], dev(-1, 0, 0, co))

    for i in range(CHUNKS):

        @pl.when(jnp.logical_not(same))
        def _():
            arrived(chunk(A0, i), sw_r.at[i])

        over_z(i, (A0, A0), AM1, AP1)

    perm = lambda xx: 2 * lax.rem(xx, 2) + xx // 2
    z_of = [PLACE[a][0] for a in range(8)]
    x_of = [PLACE[a][1] for a in range(8)]

    def rank(slot):
        zz = lax.rem(z + pick(slot, z_of) + 8, 8)
        xx = lax.rem(x + pick(slot, x_of) + 4, 4)
        return 4 * zz + perm(xx)

    def task(t):
        first = pick(t, [a for a, _ in TASKS])
        second = pick(t, [AP2 if b is None else b for _, b in TASKS])
        second = jnp.where((t == N - 1) & (x >= 2), AM2, second)
        ahead = lax.rem(rank(first) - rank(second) + 32, 32)
        swapped = ahead > 16
        left = jnp.where(swapped, second, first)
        right = jnp.where(swapped, first, second)
        return left, right, jnp.where(swapped, 32 - ahead, ahead)

    def core_copy(t):
        theirs = pl.ds(pl.multiple_of(128 * (1 - co), 128), 128)
        return send(prod.at[t, theirs], core_in.at[t], core_s.at[t], core_r.at[t], at(core_row, col))

    def compute(t):
        left, right, _ = task(t)
        prod[t] = lax.dot_general(
            pan[left], pan[right], (((1,), (1,)), ((), ())), preferred_element_type=jnp.float32
        )

    def y_copy(t, k):
        to = lax.rem(y + k, 4)
        rows = pl.ds(pl.multiple_of(32 * to, 32), 32)
        return send(half.at[t, rows], y_in.at[t, k - 1], y_s.at[t, k - 1], y_r.at[t, k - 1], dev(0, 0, k, co))

    def add_cores(t):
        arrived(core_in.at[t], core_r.at[t])
        half[t] = prod[t, pl.ds(pl.multiple_of(128 * co, 128), 128)] + core_in[t]
        for k in (2, 1, 3):
            y_copy(t, k).start()

    part = 4 * co + y
    rows_of_part = pl.ds(pl.multiple_of(32 * part, 32), 32)

    def target(t):
        left, _, ahead = task(t)
        to_row = rank(left)
        to_col = jnp.where(ahead == 0, part, (ahead - 1) // 2)
        return to_row, to_col, lax.rem(ahead + 1, 2), (to_row == row) & (to_col == col)

    def add_y(t, diagonal):
        for k in range(3):
            arrived(y_in.at[t, k], y_r.at[t, k])
        mine = half[t, pl.ds(pl.multiple_of(32 * y, 32), 32)]
        piece[t] = (mine + y_in[t, 1]) + (y_in[t, 0] + y_in[t, 2])
        to_row, to_col, slot, here = target(t)
        dst = fin_diag if diagonal else fin.at[slot, rows_of_part]
        r_sem = find_r.at[0] if diagonal else fin_r.at[slot, part]

        @pl.when(here)
        def _():
            pltpu.make_async_copy(piece.at[t], dst, r_sem).start()

        @pl.when(jnp.logical_not(here))
        def _():
            send(piece.at[t], dst, fin_s.at[t], r_sem, at(to_row, to_col)).start()

    def run(phase):
        @pl.loop(PHASES[phase], PHASES[phase + 1])
        def _(t):
            compute(t)
            core_copy(t).start()

    def reduce_cores(first, last):
        @pl.loop(first, last)
        def _(t):
            add_cores(t)

    def reduce_y(first, last):
        @pl.loop(first, last)
        def _(t):
            add_y(t, False)

    run(0)
    for i in range(CHUNKS):
        arrived(chunk(AM1, i), pan_r.at[AM1, i])
        arrived(chunk(AP1, i), pan_r.at[AP1, i])
        over_z(i, (AM1, AP1), AM2, AP2)
        if i == 0:
            add_cores(0)
        if i == 1:
            add_y(0, True)
    run(1)

    def last_panel(i):
        if i % 2:
            source, device = XM, dev(0, 1, 0, co)
        else:
            source, device = XP, dev(0, -1, 0, co)
        for slot in (XP, XM):
            arrived(chunk(slot, i), pan_r.at[slot, i])
        start(chunk(source, i), chunk(XX, i), pan_s.at[XX, i], pan_r.at[XX, i], device)

    for i in range(CHUNKS):
        arrived(chunk(AP2, i), pan_r.at[AP2, i])
        start(chunk(AP2, i), chunk(XP, i), pan_s.at[XP, i], pan_r.at[XP, i], dev(0, -1, 0, co))
        start(chunk(AP2, i), chunk(XM, i), pan_s.at[XM, i], pan_r.at[XM, i], dev(0, 1, 0, co))
        if i == 0:
            reduce_cores(1, 3)
        if i == 1:
            reduce_y(1, 3)
        if i >= 1:
            last_panel(i - 1)
    for i in range(CHUNKS):
        arrived(chunk(AM2, i), pan_r.at[AM2, i])
    run(2)
    reduce_cores(3, 5)
    last_panel(CHUNKS - 1)
    run(3)
    reduce_cores(5, 13)
    reduce_y(3, 9)
    for i in range(CHUNKS):
        arrived(chunk(XX, i), pan_r.at[XX, i])
    run(4)
    reduce_cores(13, 17)
    reduce_y(9, 17)

    arrived(fin_diag, find_r.at[0])
    diag_out[...] = DECAY * diag_ref[...] + (1.0 - DECAY) * fin_diag[...]
    for slot in range(2):
        for k in range(8):
            arrived(fin.at[slot, pl.ds(32 * k, 32)], fin_r.at[slot, k])
        band_out[:, slot, :] = DECAY * band_ref[:, slot, :] + (1.0 - DECAY) * fin[slot]

    for copy in sent:
        copy.wait_send()

    @pl.when(jnp.logical_not(same))
    def _():
        for i in range(CHUNKS):
            swap(i).wait_send()

    @pl.loop(0, N)
    def _(t):
        core_copy(t).wait_send()
        for k in range(1, 4):
            y_copy(t, k).wait_send()
        to_row, to_col, slot, here = target(t)

        @pl.when(jnp.logical_not(here))
        def _():
            send(piece.at[t], fin_diag, fin_s.at[t], find_r.at[0], at(to_row, to_col)).wait_send()


def body(activations, cotangent, accumulated, band_old, diagonal_old):
    dma = pltpu.SemaphoreType.DMA
    f32, bf16 = jnp.float32, jnp.bfloat16
    vmem = pl.BlockSpec(memory_space=pltpu.VMEM)
    return pl.pallas_call(
        kernel,
        out_shape=(
            jax.ShapeDtypeStruct(band_old.shape, f32),
            jax.ShapeDtypeStruct(diagonal_old.shape, f32),
        ),
        in_specs=[vmem] * 5,
        out_specs=(vmem, vmem),
        scratch_shapes=[
            pltpu.VMEM((512, 256), bf16),
            pltpu.VMEM((512, 1792), bf16),
            pltpu.VMEM((9, 256, 1792), bf16),
            pltpu.VMEM((N, 256, 256), f32),
            pltpu.VMEM((N, 128, 256), f32),
            pltpu.VMEM((N, 128, 256), f32),
            pltpu.VMEM((N, 3, 32, 256), f32),
            pltpu.VMEM((N, 32, 256), f32),
            pltpu.VMEM((2, 256, 256), f32),
            pltpu.VMEM((32, 256), f32),
            dma((8,)), dma((8,)), dma((8,)), dma((8,)), dma((8,)), dma((8,)), dma((16,)), dma((16,)),
            dma((CHUNKS,)), dma((CHUNKS,)), dma((8, CHUNKS)), dma((8, CHUNKS)),
            dma((N,)), dma((N,)), dma((N, 3)), dma((N, 3)), dma((N,)), dma((2, 8)), dma((1,)),
        ],
        compiler_params=pltpu.CompilerParams(
            collective_id=0, has_side_effects=True, vmem_limit_bytes=56 * 2**20
        ),
    )(activations, cotangent, accumulated, band_old, diagonal_old)


def solution(mesh):
    in_specs = (
        P("col", "row"),
        P("row", "col"),
        P("row", "col"),
        P("row", "col", None),
        P(("row", "col"), None),
    )
    out_specs = (P("row", "col", None), P(("row", "col"), None))
    return jax.shard_map(body, mesh=mesh, in_specs=in_specs, out_specs=out_specs, check_vma=False)
```

```python
import jax
import jax.numpy as jnp
from jax import lax
from jax.experimental import pallas as pl
from jax.experimental.pallas import tpu as pltpu
from jax.sharding import PartitionSpec as P

MESH = pl.DeviceIdType.MESH
DECAY = 0.95
CHUNKS = 8
GROUPS = 2
LEAD = 4

A0, AM1, AP1, AM2, AP2, XP, XM, XX, STAGE = range(9)
PLACE = ((0, 0), (-1, 0), (1, 0), (-2, 0), (2, 0), (-2, 1), (-2, -1), (-2, 2))
TASKS = (
    (A0, A0), (A0, AM1), (AP1, AM1),
    (AP1, AM2), (AP1, XP), (A0, XP), (AM1, XP), (AP1, XM), (A0, XM), (AM1, XM),
    (AP1, XX), (A0, XX), (AM1, XX),
    (AP2, AM2), (None, XP), (None, XM), (None, XX),
)
N = len(TASKS)
UNITS = (
    ((0, 1, None), (1, 2, None))
    + tuple((3, 7, g) for g in range(GROUPS))
    + tuple((10, 3, g) for g in range(GROUPS))
    + ((13, 3, None), (16, 1, None))
)


def pick(index, values):
    result = jnp.int32(values[0])
    for i, value in enumerate(values):
        if i and value != values[0]:
            result = jnp.where(index == i, jnp.int32(value), result)
    return result


def kernel(
    act_ref, cot_ref, acc_ref, band_ref, diag_ref, band_out, diag_out,
    act_all, act_t, cot_all, pan, prod, core_in, half, y_in, piece, fin, fin_diag,
    act_s, act_r, cz_s, cz_r, cx_s, cx_r, cc_s, cc_r, sw_s, sw_r, pan_s, pan_r,
    core_s, core_r, y_s, y_r, fin_s, fin_r, find_s, find_r,
):
    row = lax.axis_index("row")
    col = lax.axis_index("col")
    z, xl, co = row // 4, lax.rem(row // 2, 2), lax.rem(row, 2)
    y, xh = col // 2, lax.rem(col, 2)
    x = 2 * xh + xl

    def at(row_, col_):
        return {"row": row_, "col": col_}

    def dev(dz, dx, dy, core):
        zz, xx, yy = lax.rem(z + dz + 8, 8), lax.rem(x + dx + 4, 4), lax.rem(y + dy + 4, 4)
        return at(4 * zz + 2 * lax.rem(xx, 2) + core, 2 * yy + xx // 2)

    def send(src, dst, s_sem, r_sem, device):
        return pltpu.make_async_remote_copy(
            src_ref=src, dst_ref=dst, send_sem=s_sem, recv_sem=r_sem, device_id=device, device_id_type=MESH
        )

    def arrived(dst, sem):
        pltpu.make_async_copy(dst, dst, sem).wait()

    sent = []

    def start(*args):
        copy = send(*args)
        copy.start()
        sent.append(copy)

    up, down = at(lax.rem(row + 4, 32), col), at(lax.rem(row + 28, 32), col)
    col_peers = [at(row, lax.rem(col + k, 8)) for k in range(1, 8)]
    core_row = row + 1 - 2 * co
    xl_row = row + 2 - 4 * xl
    other_col = col + 1 - 2 * xh
    barrier = pltpu.get_barrier_semaphore()
    greet = [up, down] + col_peers + [at(core_row, col), at(xl_row, col), at(xl_row, other_col), at(core_row, other_col)]
    for peer in greet:
        pl.semaphore_signal(barrier, inc=1, device_id=peer, device_id_type=MESH)
    pl.semaphore_wait(barrier, len(greet))

    def cot_piece(row_):
        return cot_all.at[pl.ds(pl.multiple_of(16 * row_, 16), 16)]

    def act_piece(col_):
        return act_all.at[pl.ds(pl.multiple_of(64 * col_, 64), 64)]

    order = (1, 7, 2, 6, 3, 5, 4)
    start(cot_ref, cot_piece(row), cz_s.at[1], cz_r.at[1], up)
    start(cot_ref, cot_piece(row), cz_s.at[7], cz_r.at[7], down)
    start(cot_ref, cot_piece(row), cx_s.at[0], cx_r.at[0], at(xl_row, col))
    start(cot_ref, cot_piece(row), cc_s.at[0], cc_r.at[0], at(core_row, col))
    for k in range(1, 8):
        start(act_ref, act_piece(col), act_s.at[k], act_r.at[k], at(row, lax.rem(col + k, 8)))
    cot_piece(row)[...] = cot_ref[...]
    act_piece(col)[...] = act_ref[...]

    def over_core(rows_of, k, slot, sems):
        source = lax.rem(rows_of - 4 * k + 32, 32)
        arrived(cot_piece(source), sems.at[k])
        start(cot_piece(source), cot_piece(source), cc_s.at[slot], cc_r.at[slot], at(core_row, col))

    for n, k in enumerate(order):
        source = lax.rem(row - 4 * k + 32, 32)
        arrived(cot_piece(source), cz_r.at[k])
        if k < 4:
            start(cot_piece(source), cot_piece(source), cz_s.at[k + 1], cz_r.at[k + 1], up)
        if k > 5:
            start(cot_piece(source), cot_piece(source), cz_s.at[k - 1], cz_r.at[k - 1], down)
        start(cot_piece(source), cot_piece(source), cx_s.at[k], cx_r.at[k], at(xl_row, col))
        start(cot_piece(source), cot_piece(source), cc_s.at[k], cc_r.at[k], at(core_row, col))
        if n == 2:
            for m in range(1, 8):
                arrived(act_piece(lax.rem(col - m + 8, 8)), act_r.at[m])
            act_t[...] = act_all[...].T
        if n > 2:
            over_core(xl_row, ((0,) + order)[n - 3], 8 + ((0,) + order)[n - 3], cx_r)
    for k in order[3:]:
        over_core(xl_row, k, 8 + k, cx_r)
    for k in (0,) + order:
        arrived(cot_piece(lax.rem(core_row - 4 * k + 32, 32)), cc_r.at[k])
    for k in (0,) + order:
        arrived(cot_piece(lax.rem(core_row + 2 - 4 * xl - 4 * k + 32, 32)), cc_r.at[8 + k])

    same = xh == co
    own = jnp.where(same, A0, STAGE)
    size = 256 // CHUNKS

    def chunk(slot, i):
        return pan.at[slot, pl.ds(size * i, size)]

    def swap(i):
        return send(chunk(STAGE, i), chunk(A0, i), sw_s.at[i], sw_r.at[i], at(4 * z + 2 * xl + xh, 2 * y + co))

    def go_up(i, source, to):
        return send(chunk(source, i), chunk(to, i), pan_s.at[to, i], pan_r.at[to, i], up)

    def go_down(i, source, to):
        return send(chunk(source, i), chunk(to, i), pan_s.at[to, i], pan_r.at[to, i], down)

    def own_over_z(i):
        if i < LEAD:
            go_up(i, A0, AM1).start()
        go_down(i, A0, AP1).start()

    tall = 128
    per = CHUNKS * tall // 256
    for j in range(256 // tall):
        rows = pl.ds(tall * j, tall)

        @pl.loop(0, 7)
        def _(n):
            columns = pl.ds(pl.multiple_of(256 * n, 256), 256)
            product = jnp.dot(act_t[rows, :], cot_all[:, columns], preferred_element_type=jnp.float32)
            pan[own, rows, columns] = (product + acc_ref[rows, columns].astype(jnp.float32)).astype(jnp.bfloat16)

        @pl.when(jnp.logical_not(same))
        def _():
            for i in range(per * j, per * (j + 1)):
                swap(i).start()

        @pl.when(same)
        def _():
            for i in range(per * j, per * (j + 1)):
                own_over_z(i)

    @pl.when(jnp.logical_not(same))
    def _():
        for i in range(CHUNKS):
            arrived(chunk(A0, i), sw_r.at[i])
            own_over_z(i)

    for i in range(CHUNKS):
        sent.extend((go_up(i, A0, AM1), go_down(i, A0, AP1)))

    firsts = [AP2 if a is None else a for a, _ in TASKS]
    seconds = [b for _, b in TASKS]

    def rank_of(dz, dx):
        zz, xx = lax.rem(z + dz + 8, 8), lax.rem(x + dx + 4, 4)
        return 4 * zz + 2 * lax.rem(xx, 2) + xx // 2

    ranks = [rank_of(*place) for place in PLACE]

    def either(t):
        return xh == 1 if t == 16 else xl == 1

    def block_of(t):
        first, second = TASKS[t]
        left = ranks[AP2] if first is None else ranks[first]
        right = ranks[second]
        if first is None:
            left = jnp.where(either(t), ranks[AM2], left)
        if t == 13:
            left, right = jnp.where(xl == 1, right, left), jnp.where(xl == 1, left, right)
        ahead = lax.rem(left - right + 32, 32)
        to_col = (ahead - 1) // 2
        return left, to_col, lax.rem(ahead + 1, 2)

    blocks = [None] + [block_of(t) for t in range(1, N)]

    def task(t):
        other = ((t >= 13) & (t <= 15)) & (xl == 1) | (t == 16) & (xh == 1)
        left = jnp.where(other, AM2, pick(t, firsts))
        return left, jnp.where((t == 13) & (xl == 1), AP2, pick(t, seconds))

    def span(u):
        t, n, g = UNITS[u]
        return pl.ds(t, n), pl.ds(0, GROUPS) if g is None else pl.ds(g, 1)

    def core_copy(u):
        tasks, groups = span(u)
        return send(
            prod.at[tasks, groups, pl.ds(pl.multiple_of(128 * (1 - co), 128), 128)], core_in.at[tasks, groups],
            core_s.at[u], core_r.at[u], at(core_row, col),
        )

    def compute(u):
        first_task, count, g = UNITS[u]

        @pl.loop(first_task, first_task + count)
        def _(t):
            left, right = task(t)
            dims = (((1,), (1,)), ((), ()))
            if g is None:
                block = lax.dot_general(pan[left], pan[right], dims, preferred_element_type=jnp.float32)
                prod[t, 0] = block[:, :128]
                prod[t, 1] = block[:, 128:]
            else:
                columns = pan[right, pl.ds(128 * g, 128)]
                prod[t, g] = lax.dot_general(pan[left], columns, dims, preferred_element_type=jnp.float32)

        start_again(core_copy(u))

    def start_again(copy):
        copy.start()
        sent.append(copy)

    def add_cores(u):
        tasks, groups = span(u)
        arrived(core_in.at[tasks, groups], core_r.at[u])
        half[tasks, groups] = prod[tasks, groups, pl.ds(pl.multiple_of(128 * co, 128), 128)] + core_in[tasks, groups]
        for k in (2, 1, 3):
            to = lax.rem(y + k, 4)
            start_again(send(
                half.at[tasks, groups, pl.ds(pl.multiple_of(32 * to, 32), 32)], y_in.at[k - 1, tasks, groups],
                y_s.at[u, k - 1], y_r.at[u, k - 1], dev(0, 0, k, co),
            ))

    part = 4 * co + y
    rows_of_part = pl.ds(pl.multiple_of(32 * part, 32), 32)

    def deliver(src, dst, s_sem, r_sem, to_row, to_col, begin):
        here = (to_row == row) & (to_col == col)
        if begin:

            @pl.when(here)
            def _():
                pltpu.make_async_copy(src, dst, r_sem).start()

        @pl.when(jnp.logical_not(here))
        def _():
            copy = send(src, dst, s_sem, r_sem, at(to_row, to_col))
            if begin:
                copy.start()
            else:
                copy.wait_send()

    def deliver_diagonal(begin):
        deliver(piece.at[0], fin_diag, find_s.at[0], find_r.at[0], ranks[A0], part, begin)

    def deliver_block(t, g, begin):
        to_row, to_col, slot = blocks[t]
        deliver(
            piece.at[t, g], fin.at[slot, g, rows_of_part], fin_s.at[t, g], fin_r.at[slot, g, part],
            to_row, to_col, begin,
        )

    def add_y(u):
        tasks, groups = span(u)
        for k in range(3):
            arrived(y_in.at[k, tasks, groups], y_r.at[u, k])
        mine = half[tasks, groups, pl.ds(pl.multiple_of(32 * y, 32), 32)]
        piece[tasks, groups] = (mine + y_in[1, tasks, groups]) + (y_in[0, tasks, groups] + y_in[2, tasks, groups])

    def finish(u):
        first_task, count, group = UNITS[u]

        for t in range(first_task, first_task + count):
            for g in range(GROUPS):
                if group is None or group == g:
                    deliver_block(t, g, True)

    def last_panel(i):
        for slot in (XP, XM):
            arrived(chunk(slot, i), pan_r.at[slot, i])
        source, device = (XM, dev(0, 1, 0, co)) if i % 2 else (XP, dev(0, -1, 0, co))
        start(chunk(source, i), chunk(XX, i), pan_s.at[XX, i], pan_r.at[XX, i], device)

    def last_arrived(i):
        arrived(chunk(XX, i), pan_r.at[XX, i])

    def arm(k):
        arrived(chunk(AM2, k), pan_r.at[AM2, k])
        start(chunk(AM2, k), chunk(XP, k), pan_s.at[XP, k], pan_r.at[XP, k], dev(0, -1, 0, co))
        start(chunk(AM2, k), chunk(XM, k), pan_s.at[XM, k], pan_r.at[XM, k], dev(0, 1, 0, co))
        if k >= 1:
            last_panel(k - 1)

    compute(0)
    for i in range(CHUNKS):
        if i >= LEAD:
            arm(i - LEAD)
        arrived(chunk(AM1, i), pan_r.at[AM1, i])
        start_again(go_up(i, AM1, AM2))
        if i + LEAD < CHUNKS:
            go_up(i + LEAD, A0, AM1).start()
        arrived(chunk(AP1, i), pan_r.at[AP1, i])
        start_again(go_down(i, AP1, AP2))
        if i == 1:
            add_cores(0)
        if i == 4:
            add_y(0)
            deliver_diagonal(True)
    compute(1)
    for k in range(CHUNKS - LEAD, CHUNKS):
        arm(k)
        if k == max(3, CHUNKS - LEAD):
            add_cores(1)
        if k == 4:
            compute(2)
        if k == 5:
            add_cores(2)
            add_y(1)
            finish(1)
            for i in range(4):
                last_arrived(i)
            compute(4)
        if k == 6:
            add_cores(4)
            add_y(2)
            finish(2)
        if k == 7:
            add_y(4)
            finish(4)
    last_panel(CHUNKS - 1)
    compute(3)
    for i in range(CHUNKS):
        arrived(chunk(AP2, i), pan_r.at[AP2, i])
    compute(6)
    add_cores(3)
    for i in range(4, CHUNKS):
        last_arrived(i)
    compute(5)
    compute(7)
    add_cores(6)
    add_y(3)
    finish(3)
    add_cores(5)
    add_cores(7)
    add_y(6)
    finish(6)
    add_y(5)
    finish(5)
    add_y(7)
    finish(7)

    arrived(fin_diag, find_r.at[0])
    for g in range(GROUPS):
        lanes = pl.ds(128 * g, 128)
        diag_out[:, lanes] = DECAY * diag_ref[:, lanes] + (1.0 - DECAY) * fin_diag[g]
    for slot in range(2):
        for k in range(8):
            for g in range(GROUPS):
                arrived(fin.at[slot, g, pl.ds(32 * k, 32)], fin_r.at[slot, g, k])
        for g in range(GROUPS):
            lanes = pl.ds(128 * g, 128)
            band_out[:, slot, lanes] = DECAY * band_ref[:, slot, lanes] + (1.0 - DECAY) * fin[slot, g]

    for copy in sent:
        copy.wait_send()

    @pl.when(jnp.logical_not(same))
    def _():
        for i in range(CHUNKS):
            swap(i).wait_send()

    deliver_diagonal(False)

    for t in range(1, N):
        for g in range(GROUPS):
            deliver_block(t, g, False)


def body(activations, cotangent, accumulated, band_old, diagonal_old):
    dma = pltpu.SemaphoreType.DMA
    f32, bf16 = jnp.float32, jnp.bfloat16
    vmem = pl.BlockSpec(memory_space=pltpu.VMEM)
    return pl.pallas_call(
        kernel,
        out_shape=(
            jax.ShapeDtypeStruct(band_old.shape, f32),
            jax.ShapeDtypeStruct(diagonal_old.shape, f32),
        ),
        in_specs=[vmem] * 5,
        out_specs=(vmem, vmem),
        scratch_shapes=[
            pltpu.VMEM((512, 256), bf16),
            pltpu.VMEM((256, 512), bf16),
            pltpu.VMEM((512, 1792), bf16),
            pltpu.VMEM((9, 256, 1792), bf16),
            pltpu.VMEM((N, GROUPS, 256, 128), f32),
            pltpu.VMEM((N, GROUPS, 128, 128), f32),
            pltpu.VMEM((N, GROUPS, 128, 128), f32),
            pltpu.VMEM((3, N, GROUPS, 32, 128), f32),
            pltpu.VMEM((N, GROUPS, 32, 128), f32),
            pltpu.VMEM((2, GROUPS, 256, 128), f32),
            pltpu.VMEM((GROUPS, 32, 128), f32),
            dma((8,)), dma((8,)), dma((8,)), dma((8,)), dma((8,)), dma((8,)), dma((16,)), dma((16,)),
            dma((CHUNKS,)), dma((CHUNKS,)), dma((8, CHUNKS)), dma((8, CHUNKS)),
            dma((len(UNITS),)), dma((len(UNITS),)), dma((len(UNITS), 3)), dma((len(UNITS), 3)),
            dma((N, GROUPS)), dma((2, GROUPS, 8)), dma((1,)), dma((1,)),
        ],
        compiler_params=pltpu.CompilerParams(
            collective_id=0, has_side_effects=True, vmem_limit_bytes=56 * 2**20
        ),
    )(activations, cotangent, accumulated, band_old, diagonal_old)


def solution(mesh):
    in_specs = (
        P("col", "row"),
        P("row", "col"),
        P("row", "col"),
        P("row", "col", None),
        P(("row", "col"), None),
    )
    out_specs = (P("row", "col", None), P(("row", "col"), None))
    return jax.shard_map(body, mesh=mesh, in_specs=in_specs, out_specs=out_specs, check_vma=False)
```

```python
import jax
import jax.numpy as jnp
from jax import lax
from jax.experimental import pallas as pl
from jax.experimental.pallas import tpu as pltpu
from jax.sharding import PartitionSpec as P

MESH = pl.DeviceIdType.MESH
DECAY = 0.95
CHUNKS = 8
GROUPS = 2
LEAD = 4

A0, AM1, AP1, AM2, AP2, XP, XM, XX, STAGE = range(9)
PLACE = ((0, 0), (-1, 0), (1, 0), (-2, 0), (2, 0), (-2, 1), (-2, -1), (-2, 2))
TASKS = (
    (A0, A0), (A0, AM1), (AP1, AM1),
    (AP1, AM2), (AP1, XP), (A0, XP), (AM1, XP), (AP1, XM), (A0, XM), (AM1, XM),
    (AP1, XX), (A0, XX), (AM1, XX),
    (AP2, AM2), (None, XP), (None, XM), (None, XX),
)
N = len(TASKS)
UNITS = (
    (0, 1, None), (1, 2, None),
    (3, 3, 0), (3, 1, 1), (10, 3, 0), (10, 3, 1),
    (13, 1, None), (16, 1, 1), (4, 6, 1), (14, 2, 1), (14, 3, 0), (6, 4, 0),
)


def pick(index, values):
    result = jnp.int32(values[0])
    for i, value in enumerate(values):
        if i and value != values[0]:
            result = jnp.where(index == i, jnp.int32(value), result)
    return result


def kernel(
    act_ref, cot_ref, acc_ref, band_ref, diag_ref, band_out, diag_out,
    act_all, act_t, cot_all, pan, prod, core_in, half, y_in, piece, fin, fin_diag,
    act_s, act_r, cz_s, cz_r, cx_s, cx_r, cc_s, cc_r, sw_s, sw_r, pan_s, pan_r,
    core_s, core_r, y_s, y_r, fin_s, fin_r, find_s, find_r,
):
    row = lax.axis_index("row")
    col = lax.axis_index("col")
    z, xl, co = row // 4, lax.rem(row // 2, 2), lax.rem(row, 2)
    y, xh = col // 2, lax.rem(col, 2)
    x = 2 * xh + xl

    def at(row_, col_):
        return {"row": row_, "col": col_}

    def dev(dz, dx, dy, core):
        zz, xx, yy = lax.rem(z + dz + 8, 8), lax.rem(x + dx + 4, 4), lax.rem(y + dy + 4, 4)
        return at(4 * zz + 2 * lax.rem(xx, 2) + core, 2 * yy + xx // 2)

    def send(src, dst, s_sem, r_sem, device):
        return pltpu.make_async_remote_copy(
            src_ref=src, dst_ref=dst, send_sem=s_sem, recv_sem=r_sem, device_id=device, device_id_type=MESH
        )

    def arrived(dst, sem):
        pltpu.make_async_copy(dst, dst, sem).wait()

    sent = []

    def start(*args):
        copy = send(*args)
        copy.start()
        sent.append(copy)

    up, down = at(lax.rem(row + 4, 32), col), at(lax.rem(row + 28, 32), col)
    col_peers = [at(row, lax.rem(col + k, 8)) for k in range(1, 8)]
    up_2, down_2 = at(lax.rem(row + 8, 32), col), at(lax.rem(row + 24, 32), col)
    core_row = row + 1 - 2 * co
    xl_row = row + 2 - 4 * xl
    other_col = col + 1 - 2 * xh
    barrier = pltpu.get_barrier_semaphore()
    greet = [up, down, up_2, down_2] + col_peers + [at(core_row, col), at(xl_row, col), at(xl_row, other_col), at(core_row, other_col)]
    for peer in greet:
        pl.semaphore_signal(barrier, inc=1, device_id=peer, device_id_type=MESH)
    pl.semaphore_wait(barrier, len(greet))

    def cot_piece(row_):
        return cot_all.at[pl.ds(pl.multiple_of(16 * row_, 16), 16)]

    def act_piece(col_):
        return act_all.at[pl.ds(pl.multiple_of(64 * col_, 64), 64)]

    order = (1, 7, 2, 6, 3, 5, 4)
    start(cot_ref, cot_piece(row), cz_s.at[1], cz_r.at[1], up)
    start(cot_ref, cot_piece(row), cz_s.at[7], cz_r.at[7], down)
    start(cot_ref, cot_piece(row), cz_s.at[2], cz_r.at[2], up_2)
    start(cot_ref, cot_piece(row), cz_s.at[6], cz_r.at[6], down_2)
    start(cot_ref, cot_piece(row), cx_s.at[0], cx_r.at[0], at(xl_row, col))
    start(cot_ref, cot_piece(row), cc_s.at[0], cc_r.at[0], at(core_row, col))
    for k in range(1, 8):
        start(act_ref, act_piece(col), act_s.at[k], act_r.at[k], at(row, lax.rem(col + k, 8)))
    cot_piece(row)[...] = cot_ref[...]
    act_piece(col)[...] = act_ref[...]

    onward = {1: (3, up_2), 2: (4, up_2), 7: (5, down_2)}

    def beside(k):
        piece_in = cot_piece(lax.rem(xl_row - 4 * k + 32, 32))
        arrived(piece_in, cx_r.at[k])
        start(piece_in, piece_in, cc_s.at[8 + k], cc_r.at[8 + k], at(core_row, col))

    after = {1: (0,), 7: (), 2: (1,), 6: (7,), 3: (2,), 5: (6,), 4: (3, 5, 4)}
    for k in order:
        piece_in = cot_piece(lax.rem(row - 4 * k + 32, 32))
        arrived(piece_in, cz_r.at[k])
        if k in onward:
            start(piece_in, piece_in, cz_s.at[onward[k][0]], cz_r.at[onward[k][0]], onward[k][1])
        start(piece_in, piece_in, cx_s.at[k], cx_r.at[k], at(xl_row, col))
        start(piece_in, piece_in, cc_s.at[k], cc_r.at[k], at(core_row, col))
        for other in after[k]:
            beside(other)
        if k == 6:
            for m in range(1, 8):
                arrived(act_piece(lax.rem(col - m + 8, 8)), act_r.at[m])
            act_t[...] = act_all[...].T
    for k in (0,) + order:
        arrived(cot_piece(lax.rem(core_row - 4 * k + 32, 32)), cc_r.at[k])
    for k in (0,) + order:
        arrived(cot_piece(lax.rem(core_row + 2 - 4 * xl - 4 * k + 32, 32)), cc_r.at[8 + k])

    same = xh == co
    own = jnp.where(same, A0, STAGE)
    size = 256 // CHUNKS

    def chunk(slot, i):
        return pan.at[slot, pl.ds(size * i, size)]

    def swap(i):
        return send(chunk(STAGE, i), chunk(A0, i), sw_s.at[i], sw_r.at[i], at(4 * z + 2 * xl + xh, 2 * y + co))

    def go_up(i, source, to):
        return send(chunk(source, i), chunk(to, i), pan_s.at[to, i], pan_r.at[to, i], up)

    def go_down(i, source, to):
        return send(chunk(source, i), chunk(to, i), pan_s.at[to, i], pan_r.at[to, i], down)

    def own_over_z(i):
        if i < LEAD:
            go_up(i, A0, AM1).start()
        go_down(i, A0, AP1).start()

    tall = 128
    per = CHUNKS * tall // 256
    for j in range(256 // tall):
        rows = pl.ds(tall * j, tall)

        @pl.loop(0, 7)
        def _(n):
            columns = pl.ds(pl.multiple_of(256 * n, 256), 256)
            product = jnp.dot(act_t[rows, :], cot_all[:, columns], preferred_element_type=jnp.float32)
            pan[own, rows, columns] = (product + acc_ref[rows, columns].astype(jnp.float32)).astype(jnp.bfloat16)

        @pl.when(jnp.logical_not(same))
        def _():
            for i in range(per * j, per * (j + 1)):
                swap(i).start()

        @pl.when(same)
        def _():
            for i in range(per * j, per * (j + 1)):
                own_over_z(i)

    @pl.when(jnp.logical_not(same))
    def _():
        for i in range(CHUNKS):
            arrived(chunk(A0, i), sw_r.at[i])
            own_over_z(i)

    for i in range(CHUNKS):
        sent.extend((go_up(i, A0, AM1), go_down(i, A0, AP1)))

    firsts = [AP2 if a is None else a for a, _ in TASKS]
    seconds = [b for _, b in TASKS]

    def rank_of(dz, dx):
        zz, xx = lax.rem(z + dz + 8, 8), lax.rem(x + dx + 4, 4)
        return 4 * zz + 2 * lax.rem(xx, 2) + xx // 2

    ranks = [rank_of(*place) for place in PLACE]

    def either(t):
        return xh == 1 if t == 16 else xl == 1

    def block_of(t):
        first, second = TASKS[t]
        left = ranks[AP2] if first is None else ranks[first]
        right = ranks[second]
        if first is None:
            left = jnp.where(either(t), ranks[AM2], left)
        if t == 13:
            left, right = jnp.where(xl == 1, right, left), jnp.where(xl == 1, left, right)
        ahead = lax.rem(left - right + 32, 32)
        to_col = (ahead - 1) // 2
        return left, to_col, lax.rem(ahead + 1, 2)

    blocks = [None] + [block_of(t) for t in range(1, N)]

    def task(t):
        other = ((t >= 13) & (t <= 15)) & (xl == 1) | (t == 16) & (xh == 1)
        left = jnp.where(other, AM2, pick(t, firsts))
        return left, jnp.where((t == 13) & (xl == 1), AP2, pick(t, seconds))

    def span(u):
        t, n, g = UNITS[u]
        return pl.ds(t, n), pl.ds(0, GROUPS) if g is None else pl.ds(g, 1)

    def core_copy(u):
        tasks, groups = span(u)
        return send(
            prod.at[tasks, groups, pl.ds(pl.multiple_of(128 * (1 - co), 128), 128)], core_in.at[tasks, groups],
            core_s.at[u], core_r.at[u], at(core_row, col),
        )

    def compute(u):
        first_task, count, g = UNITS[u]

        @pl.loop(first_task, first_task + count)
        def _(t):
            left, right = task(t)
            dims = (((1,), (1,)), ((), ()))
            if g is None:
                block = lax.dot_general(pan[left], pan[right], dims, preferred_element_type=jnp.float32)
                prod[t, 0] = block[:, :128]
                prod[t, 1] = block[:, 128:]
            else:
                columns = pan[right, pl.ds(128 * g, 128)]
                prod[t, g] = lax.dot_general(pan[left], columns, dims, preferred_element_type=jnp.float32)

        start_again(core_copy(u))

    def start_again(copy):
        copy.start()
        sent.append(copy)

    def add_cores(u):
        tasks, groups = span(u)
        arrived(core_in.at[tasks, groups], core_r.at[u])
        half[tasks, groups] = prod[tasks, groups, pl.ds(pl.multiple_of(128 * co, 128), 128)] + core_in[tasks, groups]
        for k in (2, 1, 3):
            to = lax.rem(y + k, 4)
            start_again(send(
                half.at[tasks, groups, pl.ds(pl.multiple_of(32 * to, 32), 32)], y_in.at[k - 1, tasks, groups],
                y_s.at[u, k - 1], y_r.at[u, k - 1], dev(0, 0, k, co),
            ))

    part = 4 * co + y
    rows_of_part = pl.ds(pl.multiple_of(32 * part, 32), 32)

    def deliver(src, dst, s_sem, r_sem, to_row, to_col, begin):
        here = (to_row == row) & (to_col == col)
        if begin:

            @pl.when(here)
            def _():
                pltpu.make_async_copy(src, dst, r_sem).start()

        @pl.when(jnp.logical_not(here))
        def _():
            copy = send(src, dst, s_sem, r_sem, at(to_row, to_col))
            if begin:
                copy.start()
            else:
                copy.wait_send()

    def deliver_diagonal(begin):
        deliver(piece.at[0], fin_diag, find_s.at[0], find_r.at[0], ranks[A0], part, begin)

    def deliver_block(t, g, begin):
        to_row, to_col, slot = blocks[t]
        deliver(
            piece.at[t, g], fin.at[slot, g, rows_of_part], fin_s.at[t, g], fin_r.at[slot, g, part],
            to_row, to_col, begin,
        )

    def add_y(u):
        tasks, groups = span(u)
        for k in range(3):
            arrived(y_in.at[k, tasks, groups], y_r.at[u, k])
        mine = half[tasks, groups, pl.ds(pl.multiple_of(32 * y, 32), 32)]
        piece[tasks, groups] = (mine + y_in[1, tasks, groups]) + (y_in[0, tasks, groups] + y_in[2, tasks, groups])

    def finish(u):
        first_task, count, group = UNITS[u]

        for t in range(first_task, first_task + count):
            for g in range(GROUPS):
                if group is None or group == g:
                    deliver_block(t, g, True)

    def last_panel(i):
        for slot in (XP, XM):
            arrived(chunk(slot, i), pan_r.at[slot, i])
        source, device = (XM, dev(0, 1, 0, co)) if i % 2 else (XP, dev(0, -1, 0, co))
        start(chunk(source, i), chunk(XX, i), pan_s.at[XX, i], pan_r.at[XX, i], device)

    def last_arrived(i):
        arrived(chunk(XX, i), pan_r.at[XX, i])

    def arm(k):
        arrived(chunk(AM2, k), pan_r.at[AM2, k])
        start(chunk(AM2, k), chunk(XP, k), pan_s.at[XP, k], pan_r.at[XP, k], dev(0, -1, 0, co))
        start(chunk(AM2, k), chunk(XM, k), pan_s.at[XM, k], pan_r.at[XM, k], dev(0, 1, 0, co))
        if k >= 1:
            last_panel(k - 1)

    compute(0)
    for i in range(CHUNKS):
        if i >= LEAD:
            arm(i - LEAD)
        arrived(chunk(AM1, i), pan_r.at[AM1, i])
        start_again(go_up(i, AM1, AM2))
        if i + LEAD < CHUNKS:
            go_up(i + LEAD, A0, AM1).start()
        arrived(chunk(AP1, i), pan_r.at[AP1, i])
        start_again(go_down(i, AP1, AP2))
        if i == 1:
            add_cores(0)
        if i == 4:
            add_y(0)
            deliver_diagonal(True)
    compute(1)
    for k in range(CHUNKS - LEAD, CHUNKS):
        arm(k)
        if k == 4:
            compute(2)
            add_cores(1)
        if k == 5:
            compute(11)
            add_cores(2)
        if k == 6:
            add_cores(11)
            for i in range(4):
                last_arrived(i)
            compute(4)
            add_y(1)
            finish(1)
        if k == 7:
            add_cores(4)
    compute(3)
    for i in range(CHUNKS):
        arrived(chunk(AP2, i), pan_r.at[AP2, i])
    compute(6)
    compute(10)
    last_panel(CHUNKS - 1)
    add_cores(3)
    add_cores(6)
    compute(8)
    add_cores(10)
    compute(9)
    add_cores(8)
    add_cores(9)
    for u in (2, 11, 4, 3, 6):
        add_y(u)
        finish(u)
    for i in range(4, CHUNKS):
        last_arrived(i)
    compute(5)
    compute(7)
    add_y(10)
    finish(10)
    add_cores(5)
    add_cores(7)
    for u in (8, 9, 5, 7):
        add_y(u)
        finish(u)

    arrived(fin_diag, find_r.at[0])
    for g in range(GROUPS):
        lanes = pl.ds(128 * g, 128)
        diag_out[:, lanes] = DECAY * diag_ref[:, lanes] + (1.0 - DECAY) * fin_diag[g]
    for slot in range(2):
        for k in range(8):
            for g in range(GROUPS):
                arrived(fin.at[slot, g, pl.ds(32 * k, 32)], fin_r.at[slot, g, k])
        for g in range(GROUPS):
            lanes = pl.ds(128 * g, 128)
            band_out[:, slot, lanes] = DECAY * band_ref[:, slot, lanes] + (1.0 - DECAY) * fin[slot, g]

    for copy in sent:
        copy.wait_send()

    @pl.when(jnp.logical_not(same))
    def _():
        for i in range(CHUNKS):
            swap(i).wait_send()

    deliver_diagonal(False)

    for t in range(1, N):
        for g in range(GROUPS):
            deliver_block(t, g, False)


def body(activations, cotangent, accumulated, band_old, diagonal_old):
    dma = pltpu.SemaphoreType.DMA
    f32, bf16 = jnp.float32, jnp.bfloat16
    vmem = pl.BlockSpec(memory_space=pltpu.VMEM)
    return pl.pallas_call(
        kernel,
        out_shape=(
            jax.ShapeDtypeStruct(band_old.shape, f32),
            jax.ShapeDtypeStruct(diagonal_old.shape, f32),
        ),
        in_specs=[vmem] * 5,
        out_specs=(vmem, vmem),
        scratch_shapes=[
            pltpu.VMEM((512, 256), bf16),
            pltpu.VMEM((256, 512), bf16),
            pltpu.VMEM((512, 1792), bf16),
            pltpu.VMEM((9, 256, 1792), bf16),
            pltpu.VMEM((N, GROUPS, 256, 128), f32),
            pltpu.VMEM((N, GROUPS, 128, 128), f32),
            pltpu.VMEM((N, GROUPS, 128, 128), f32),
            pltpu.VMEM((3, N, GROUPS, 32, 128), f32),
            pltpu.VMEM((N, GROUPS, 32, 128), f32),
            pltpu.VMEM((2, GROUPS, 256, 128), f32),
            pltpu.VMEM((GROUPS, 32, 128), f32),
            dma((8,)), dma((8,)), dma((8,)), dma((8,)), dma((8,)), dma((8,)), dma((16,)), dma((16,)),
            dma((CHUNKS,)), dma((CHUNKS,)), dma((8, CHUNKS)), dma((8, CHUNKS)),
            dma((len(UNITS),)), dma((len(UNITS),)), dma((len(UNITS), 3)), dma((len(UNITS), 3)),
            dma((N, GROUPS)), dma((2, GROUPS, 8)), dma((1,)), dma((1,)),
        ],
        compiler_params=pltpu.CompilerParams(
            collective_id=0, has_side_effects=True, vmem_limit_bytes=56 * 2**20
        ),
    )(activations, cotangent, accumulated, band_old, diagonal_old)


def solution(mesh):
    in_specs = (
        P("col", "row"),
        P("row", "col"),
        P("row", "col"),
        P("row", "col", None),
        P(("row", "col"), None),
    )
    out_specs = (P("row", "col", None), P(("row", "col"), None))
    return jax.shard_map(body, mesh=mesh, in_specs=in_specs, out_specs=out_specs, check_vma=False)
```

```python
import jax
import jax.numpy as jnp
from jax import lax
from jax.experimental import pallas as pl
from jax.experimental.pallas import tpu as pltpu
from jax.sharding import PartitionSpec as P

MESH = pl.DeviceIdType.MESH
DECAY = 0.95
CHUNKS = 8
GROUPS = 2
LEAD = 4

A0, AM1, AP1, AM2, AP2, XP, XM, XX, STAGE = range(9)
PLACE = ((0, 0), (-1, 0), (1, 0), (-2, 0), (2, 0), (-2, 1), (-2, -1), (-2, 2))
TASKS = (
    (A0, A0), (A0, AM1), (AP1, AM1),
    (AP1, AM2), (AP1, XP), (AP1, XM), (A0, XP), (A0, XM), (AM1, XP), (AM1, XM),
    (AP1, XX), (A0, XX), (AM1, XX),
    (AP2, AM2), (None, XP), (None, XM), (None, XX),
)
N = len(TASKS)
UNITS = (
    (0, 1, None), (1, 2, None),
    (3, 3, 0), (3, 1, 1), (10, 3, 0), (10, 3, 1),
    (13, 1, None), (16, 1, 1), (4, 6, 1), (14, 2, 1), (14, 3, 0), (6, 4, 0),
)


def pick(index, values):
    result = jnp.int32(values[0])
    for i, value in enumerate(values):
        if i and value != values[0]:
            result = jnp.where(index == i, jnp.int32(value), result)
    return result


def kernel(
    act_ref, cot_ref, acc_hbm, band_hbm, diag_ref, band_out, diag_out,
    acc_ref, band_ref, load_s,
    act_all, act_t, cot_all, pan, prod, core_in, half, y_in, piece, fin, fin_diag,
    act_s, act_r, cz_s, cz_r, cx_s, cx_r, cc_s, cc_r, sw_s, sw_r, pan_s, pan_r,
    core_s, core_r, y_s, y_r, fin_s, fin_r, find_s, find_r,
):
    row = lax.axis_index("row")
    col = lax.axis_index("col")
    z, xl, co = row // 4, lax.rem(row // 2, 2), lax.rem(row, 2)
    y, xh = col // 2, lax.rem(col, 2)
    x = 2 * xh + xl

    def at(row_, col_):
        return {"row": row_, "col": col_}

    def dev(dz, dx, dy, core):
        zz, xx, yy = lax.rem(z + dz + 8, 8), lax.rem(x + dx + 4, 4), lax.rem(y + dy + 4, 4)
        return at(4 * zz + 2 * lax.rem(xx, 2) + core, 2 * yy + xx // 2)

    def send(src, dst, s_sem, r_sem, device):
        return pltpu.make_async_remote_copy(
            src_ref=src, dst_ref=dst, send_sem=s_sem, recv_sem=r_sem, device_id=device, device_id_type=MESH
        )

    def arrived(dst, sem):
        pltpu.make_async_copy(dst, dst, sem).wait()

    sent = []

    def start(*args):
        copy = send(*args)
        copy.start()
        sent.append(copy)

    up, down = at(lax.rem(row + 4, 32), col), at(lax.rem(row + 28, 32), col)
    col_peers = [at(row, lax.rem(col + k, 8)) for k in range(1, 8)]
    up_2, down_2 = at(lax.rem(row + 8, 32), col), at(lax.rem(row + 24, 32), col)
    core_row = row + 1 - 2 * co
    xl_row = row + 2 - 4 * xl
    other_col = col + 1 - 2 * xh
    loads = (
        pltpu.make_async_copy(acc_hbm, acc_ref, load_s.at[0]),
        pltpu.make_async_copy(band_hbm, band_ref, load_s.at[1]),
    )
    for load in loads:
        load.start()
    barrier = pltpu.get_barrier_semaphore()
    greet = [up, down, up_2, down_2] + col_peers + [at(core_row, col), at(xl_row, col), at(xl_row, other_col), at(core_row, other_col)]
    for peer in greet:
        pl.semaphore_signal(barrier, inc=1, device_id=peer, device_id_type=MESH)
    pl.semaphore_wait(barrier, len(greet))

    def cot_piece(row_):
        return cot_all.at[pl.ds(pl.multiple_of(16 * row_, 16), 16)]

    def act_piece(col_):
        return act_all.at[pl.ds(pl.multiple_of(64 * col_, 64), 64)]

    order = (1, 7, 2, 6, 3, 5, 4)
    start(cot_ref, cot_piece(row), cz_s.at[1], cz_r.at[1], up)
    start(cot_ref, cot_piece(row), cz_s.at[7], cz_r.at[7], down)
    start(cot_ref, cot_piece(row), cz_s.at[2], cz_r.at[2], up_2)
    start(cot_ref, cot_piece(row), cz_s.at[6], cz_r.at[6], down_2)
    start(cot_ref, cot_piece(row), cx_s.at[0], cx_r.at[0], at(xl_row, col))
    start(cot_ref, cot_piece(row), cc_s.at[0], cc_r.at[0], at(core_row, col))
    for k in range(1, 8):
        start(act_ref, act_piece(col), act_s.at[k], act_r.at[k], at(row, lax.rem(col + k, 8)))
    cot_piece(row)[...] = cot_ref[...]
    act_piece(col)[...] = act_ref[...]

    onward = {1: (3, up_2), 2: (4, up_2), 7: (5, down_2)}

    def beside(k):
        piece_in = cot_piece(lax.rem(xl_row - 4 * k + 32, 32))
        arrived(piece_in, cx_r.at[k])
        start(piece_in, piece_in, cc_s.at[8 + k], cc_r.at[8 + k], at(core_row, col))

    after = {1: (0,), 7: (), 2: (1,), 6: (7,), 3: (2,), 5: (6,), 4: (3, 5, 4)}
    for k in order:
        piece_in = cot_piece(lax.rem(row - 4 * k + 32, 32))
        arrived(piece_in, cz_r.at[k])
        if k in onward:
            start(piece_in, piece_in, cz_s.at[onward[k][0]], cz_r.at[onward[k][0]], onward[k][1])
        start(piece_in, piece_in, cx_s.at[k], cx_r.at[k], at(xl_row, col))
        start(piece_in, piece_in, cc_s.at[k], cc_r.at[k], at(core_row, col))
        for other in after[k]:
            beside(other)
        if k == 6:
            for m in range(1, 8):
                arrived(act_piece(lax.rem(col - m + 8, 8)), act_r.at[m])
            act_t[...] = act_all[...].T
    for k in (0,) + order:
        arrived(cot_piece(lax.rem(core_row - 4 * k + 32, 32)), cc_r.at[k])
    for k in (0,) + order:
        arrived(cot_piece(lax.rem(core_row + 2 - 4 * xl - 4 * k + 32, 32)), cc_r.at[8 + k])

    same = xh == co
    own = jnp.where(same, A0, STAGE)
    size = 256 // CHUNKS

    def chunk(slot, i):
        if slot in (XP, XM):
            half_of, first = divmod(size * i, 128)
            return pan.at[XP + half_of, pl.ds(first + 128 * (slot - XP), size)]
        return pan.at[slot, pl.ds(size * i, size)]

    def swap(i):
        return send(chunk(STAGE, i), chunk(A0, i), sw_s.at[i], sw_r.at[i], at(4 * z + 2 * xl + xh, 2 * y + co))

    def go_up(i, source, to):
        return send(chunk(source, i), chunk(to, i), pan_s.at[to, i], pan_r.at[to, i], up)

    def go_down(i, source, to):
        return send(chunk(source, i), chunk(to, i), pan_s.at[to, i], pan_r.at[to, i], down)

    def own_over_z(i):
        if i < LEAD:
            go_up(i, A0, AM1).start()
        go_down(i, A0, AP1).start()

    loads[0].wait()
    tall = 128
    per = CHUNKS * tall // 256
    for j in range(256 // tall):
        rows = pl.ds(tall * j, tall)

        @pl.loop(0, 7)
        def _(n):
            columns = pl.ds(pl.multiple_of(256 * n, 256), 256)
            product = jnp.dot(act_t[rows, :], cot_all[:, columns], preferred_element_type=jnp.float32)
            pan[own, rows, columns] = (product + acc_ref[rows, columns].astype(jnp.float32)).astype(jnp.bfloat16)

        @pl.when(jnp.logical_not(same))
        def _():
            for i in range(per * j, per * (j + 1)):
                swap(i).start()

        @pl.when(same)
        def _():
            for i in range(per * j, per * (j + 1)):
                own_over_z(i)

    @pl.when(jnp.logical_not(same))
    def _():
        for i in range(CHUNKS):
            arrived(chunk(A0, i), sw_r.at[i])
            own_over_z(i)

    for i in range(CHUNKS):
        sent.extend((go_up(i, A0, AM1), go_down(i, A0, AP1)))

    firsts = [AP2 if a is None else a for a, _ in TASKS]
    seconds = [b for _, b in TASKS]

    def rank_of(dz, dx):
        zz, xx = lax.rem(z + dz + 8, 8), lax.rem(x + dx + 4, 4)
        return 4 * zz + 2 * lax.rem(xx, 2) + xx // 2

    ranks = [rank_of(*place) for place in PLACE]

    def either(t):
        return xh == 1 if t == 16 else xl == 1

    def block_of(t):
        first, second = TASKS[t]
        left = ranks[AP2] if first is None else ranks[first]
        right = ranks[second]
        if first is None:
            left = jnp.where(either(t), ranks[AM2], left)
        if t == 13:
            left, right = jnp.where(xl == 1, right, left), jnp.where(xl == 1, left, right)
        ahead = lax.rem(left - right + 32, 32)
        to_col = (ahead - 1) // 2
        return left, to_col, lax.rem(ahead + 1, 2)

    blocks = [None] + [block_of(t) for t in range(1, N)]

    def task(t):
        other = ((t >= 13) & (t <= 15)) & (xl == 1) | (t == 16) & (xh == 1)
        left = jnp.where(other, AM2, pick(t, firsts))
        return left, jnp.where((t == 13) & (xl == 1), AP2, pick(t, seconds))

    def span(u):
        t, n, g = UNITS[u]
        return pl.ds(t, n), pl.ds(0, GROUPS) if g is None else pl.ds(g, 1)

    def core_copy(u):
        tasks, groups = span(u)
        return send(
            prod.at[tasks, groups, pl.ds(pl.multiple_of(128 * (1 - co), 128), 128)], core_in.at[tasks, groups],
            core_s.at[u], core_r.at[u], at(core_row, col),
        )

    def multiply(left, right):
        return lax.dot_general(
            pan[left], right, (((1,), (1,)), ((), ())), preferred_element_type=jnp.float32
        )

    def compute(u):
        first_task, count, g = UNITS[u]
        if g is None:

            @pl.loop(first_task, first_task + count)
            def _(t):
                left, right = task(t)
                block = multiply(left, pan[right])
                prod[t, 0] = block[:, :128]
                prod[t, 1] = block[:, 128:]

        else:
            t, last = first_task, first_task + count
            while t < last:
                if TASKS[t][1] == XP:
                    pairs = 1
                    while t + 2 * pairs + 1 < last and TASKS[t + 2 * pairs][1] == XP:
                        pairs += 1

                    @pl.loop(0, pairs)
                    def _(n, t=t):
                        left, _ = task(t + 2 * n)
                        block = multiply(left, pan[XP + g])
                        prod[t + 2 * n, g] = block[:, :128]
                        prod[t + 2 * n + 1, g] = block[:, 128:]

                    t += 2 * pairs
                else:
                    others = 1
                    while t + others < last and TASKS[t + others][1] != XP:
                        others += 1

                    @pl.loop(t, t + others)
                    def _(n):
                        left, right = task(n)
                        prod[n, g] = multiply(left, pan[right, pl.ds(128 * g, 128)])

                    t += others
        start_again(core_copy(u))

    def start_again(copy):
        copy.start()
        sent.append(copy)

    def add_cores(u):
        tasks, groups = span(u)
        arrived(core_in.at[tasks, groups], core_r.at[u])
        half[tasks, groups] = prod[tasks, groups, pl.ds(pl.multiple_of(128 * co, 128), 128)] + core_in[tasks, groups]
        for k in (2, 1, 3):
            to = lax.rem(y + k, 4)
            start_again(send(
                half.at[tasks, groups, pl.ds(pl.multiple_of(32 * to, 32), 32)], y_in.at[k - 1, tasks, groups],
                y_s.at[u, k - 1], y_r.at[u, k - 1], dev(0, 0, k, co),
            ))

    part = 4 * co + y
    rows_of_part = pl.ds(pl.multiple_of(32 * part, 32), 32)

    def deliver(src, dst, s_sem, r_sem, to_row, to_col, begin):
        here = (to_row == row) & (to_col == col)
        if begin:

            @pl.when(here)
            def _():
                pltpu.make_async_copy(src, dst, r_sem).start()

        @pl.when(jnp.logical_not(here))
        def _():
            copy = send(src, dst, s_sem, r_sem, at(to_row, to_col))
            if begin:
                copy.start()
            else:
                copy.wait_send()

    def deliver_diagonal(begin):
        deliver(piece.at[0], fin_diag, find_s.at[0], find_r.at[0], ranks[A0], part, begin)

    def deliver_block(t, g, begin):
        to_row, to_col, slot = blocks[t]
        deliver(
            piece.at[t, g], fin.at[slot, g, rows_of_part], fin_s.at[t, g], fin_r.at[slot, g, part],
            to_row, to_col, begin,
        )

    def add_y(u):
        tasks, groups = span(u)
        for k in range(3):
            arrived(y_in.at[k, tasks, groups], y_r.at[u, k])
        mine = half[tasks, groups, pl.ds(pl.multiple_of(32 * y, 32), 32)]
        piece[tasks, groups] = (mine + y_in[1, tasks, groups]) + (y_in[0, tasks, groups] + y_in[2, tasks, groups])

    def finish(u):
        first_task, count, group = UNITS[u]

        for t in range(first_task, first_task + count):
            for g in range(GROUPS):
                if group is None or group == g:
                    deliver_block(t, g, True)

    def last_panel(i):
        for slot in (XP, XM):
            arrived(chunk(slot, i), pan_r.at[slot, i])
        source, device = (XM, dev(0, 1, 0, co)) if i % 2 else (XP, dev(0, -1, 0, co))
        start(chunk(source, i), chunk(XX, i), pan_s.at[XX, i], pan_r.at[XX, i], device)

    def last_arrived(i):
        arrived(chunk(XX, i), pan_r.at[XX, i])

    def arm(k):
        arrived(chunk(AM2, k), pan_r.at[AM2, k])
        start(chunk(AM2, k), chunk(XP, k), pan_s.at[XP, k], pan_r.at[XP, k], dev(0, -1, 0, co))
        start(chunk(AM2, k), chunk(XM, k), pan_s.at[XM, k], pan_r.at[XM, k], dev(0, 1, 0, co))
        if k >= 1:
            last_panel(k - 1)

    compute(0)
    for i in range(CHUNKS):
        if i >= LEAD:
            arm(i - LEAD)
        arrived(chunk(AM1, i), pan_r.at[AM1, i])
        start_again(go_up(i, AM1, AM2))
        if i + LEAD < CHUNKS:
            go_up(i + LEAD, A0, AM1).start()
        arrived(chunk(AP1, i), pan_r.at[AP1, i])
        start_again(go_down(i, AP1, AP2))
        if i == 1:
            add_cores(0)
        if i == 4:
            add_y(0)
            deliver_diagonal(True)
    compute(1)
    for k in range(CHUNKS - LEAD, CHUNKS):
        arm(k)
        if k == 4:
            compute(2)
            add_cores(1)
        if k == 5:
            compute(11)
            add_cores(2)
        if k == 6:
            add_cores(11)
            for i in range(4):
                last_arrived(i)
            compute(4)
            add_y(1)
            finish(1)
        if k == 7:
            add_cores(4)
    compute(3)
    for i in range(CHUNKS):
        arrived(chunk(AP2, i), pan_r.at[AP2, i])
    compute(6)
    compute(10)
    last_panel(CHUNKS - 1)
    add_cores(3)
    add_cores(6)
    compute(8)
    add_cores(10)
    compute(9)
    add_cores(8)
    add_cores(9)
    for u in (2, 11, 4, 3, 6):
        add_y(u)
        finish(u)
    for i in range(4, CHUNKS):
        last_arrived(i)
    compute(5)
    compute(7)
    add_y(10)
    finish(10)
    add_cores(5)
    add_cores(7)
    for u in (8, 9, 5, 7):
        add_y(u)
        finish(u)

    loads[1].wait()
    arrived(fin_diag, find_r.at[0])
    for g in range(GROUPS):
        lanes = pl.ds(128 * g, 128)
        diag_out[:, lanes] = DECAY * diag_ref[:, lanes] + (1.0 - DECAY) * fin_diag[g]
    for slot in range(2):
        for k in range(8):
            for g in range(GROUPS):
                arrived(fin.at[slot, g, pl.ds(32 * k, 32)], fin_r.at[slot, g, k])
        for g in range(GROUPS):
            lanes = pl.ds(128 * g, 128)
            band_out[:, slot, lanes] = DECAY * band_ref[:, slot, lanes] + (1.0 - DECAY) * fin[slot, g]

    for copy in sent:
        copy.wait_send()

    @pl.when(jnp.logical_not(same))
    def _():
        for i in range(CHUNKS):
            swap(i).wait_send()

    deliver_diagonal(False)

    for t in range(1, N):
        for g in range(GROUPS):
            deliver_block(t, g, False)


def body(activations, cotangent, accumulated, band_old, diagonal_old):
    dma = pltpu.SemaphoreType.DMA
    f32, bf16 = jnp.float32, jnp.bfloat16
    vmem = pl.BlockSpec(memory_space=pltpu.VMEM)
    hbm = pl.BlockSpec(memory_space=pl.ANY)
    return pl.pallas_call(
        kernel,
        out_shape=(
            jax.ShapeDtypeStruct(band_old.shape, f32),
            jax.ShapeDtypeStruct(diagonal_old.shape, f32),
        ),
        in_specs=[vmem, vmem, hbm, hbm, vmem],
        out_specs=(vmem, vmem),
        scratch_shapes=[
            pltpu.VMEM(accumulated.shape, bf16),
            pltpu.VMEM(band_old.shape, f32),
            dma((2,)),
            pltpu.VMEM((512, 256), bf16),
            pltpu.VMEM((256, 512), bf16),
            pltpu.VMEM((512, 1792), bf16),
            pltpu.VMEM((9, 256, 1792), bf16),
            pltpu.VMEM((N, GROUPS, 256, 128), f32),
            pltpu.VMEM((N, GROUPS, 128, 128), f32),
            pltpu.VMEM((N, GROUPS, 128, 128), f32),
            pltpu.VMEM((3, N, GROUPS, 32, 128), f32),
            pltpu.VMEM((N, GROUPS, 32, 128), f32),
            pltpu.VMEM((2, GROUPS, 256, 128), f32),
            pltpu.VMEM((GROUPS, 32, 128), f32),
            dma((8,)), dma((8,)), dma((8,)), dma((8,)), dma((8,)), dma((8,)), dma((16,)), dma((16,)),
            dma((CHUNKS,)), dma((CHUNKS,)), dma((8, CHUNKS)), dma((8, CHUNKS)),
            dma((len(UNITS),)), dma((len(UNITS),)), dma((len(UNITS), 3)), dma((len(UNITS), 3)),
            dma((N, GROUPS)), dma((2, GROUPS, 8)), dma((1,)), dma((1,)),
        ],
        compiler_params=pltpu.CompilerParams(
            collective_id=0, has_side_effects=True, vmem_limit_bytes=56 * 2**20
        ),
    )(activations, cotangent, accumulated, band_old, diagonal_old)


def solution(mesh):
    in_specs = (
        P("col", "row"),
        P("row", "col"),
        P("row", "col"),
        P("row", "col", None),
        P(("row", "col"), None),
    )
    out_specs = (P("row", "col", None), P(("row", "col"), None))
    return jax.shard_map(body, mesh=mesh, in_specs=in_specs, out_specs=out_specs, check_vma=False)
```

```python
import jax
import jax.numpy as jnp
from jax import lax
from jax.experimental import pallas as pl
from jax.experimental.pallas import tpu as pltpu
from jax.sharding import PartitionSpec as P

MESH = pl.DeviceIdType.MESH
DECAY = 0.95
CHUNKS = 8
GROUPS = 2
LEAD = 4

A0, AM1, AP1, AM2, AP2, XP, XM, XX, STAGE = range(9)
PLACE = ((0, 0), (-1, 0), (1, 0), (-2, 0), (2, 0), (-2, 1), (-2, -1), (-2, 2))
TASKS = (
    (A0, A0), (A0, AM1), (AP1, AM1),
    (AP1, AM2), (AP1, XP), (AP1, XM), (A0, XP), (A0, XM), (AM1, XP), (AM1, XM),
    (AP1, XX), (A0, XX), (AM1, XX),
    (AP2, AM2), (None, XP), (None, XM), (None, XX),
)
N = len(TASKS)
UNITS = (
    (0, 1, None), (1, 2, None),
    (3, 3, 0), (3, 1, 1), (10, 3, 0), (10, 3, 1),
    (13, 1, None), (16, 1, 1), (4, 6, 1), (14, 2, 1), (14, 3, 0), (6, 4, 0),
)


def pick(index, values):
    result = jnp.int32(values[0])
    for i, value in enumerate(values):
        if i and value != values[0]:
            result = jnp.where(index == i, jnp.int32(value), result)
    return result


def kernel(
    act_ref, cot_ref, acc_hbm, band_hbm, diag_ref, band_out, diag_out,
    acc_ref, band_ref, load_s,
    act_all, act_t, cot_all, pan, prod, core_in, half, y_in, piece, fin, fin_diag,
    act_s, act_r, cz_s, cz_r, cx_s, cx_r, cc_s, cc_r, sw_s, sw_r, pan_s, pan_r,
    core_s, core_r, y_s, y_r, fin_s, fin_r, find_s, find_r,
):
    row = lax.axis_index("row")
    col = lax.axis_index("col")
    z, xl, co = row // 4, lax.rem(row // 2, 2), lax.rem(row, 2)
    y, xh = col // 2, lax.rem(col, 2)
    x = 2 * xh + xl

    def at(row_, col_):
        return {"row": row_, "col": col_}

    def dev(dz, dx, dy, core):
        zz, xx, yy = lax.rem(z + dz + 8, 8), lax.rem(x + dx + 4, 4), lax.rem(y + dy + 4, 4)
        return at(4 * zz + 2 * lax.rem(xx, 2) + core, 2 * yy + xx // 2)

    def send(src, dst, s_sem, r_sem, device):
        return pltpu.make_async_remote_copy(
            src_ref=src, dst_ref=dst, send_sem=s_sem, recv_sem=r_sem, device_id=device, device_id_type=MESH
        )

    def arrived(dst, sem):
        pltpu.make_async_copy(dst, dst, sem).wait()

    sent = []

    def start(*args):
        copy = send(*args)
        copy.start()
        sent.append(copy)

    up, down = at(lax.rem(row + 4, 32), col), at(lax.rem(row + 28, 32), col)
    col_peers = [at(row, lax.rem(col + k, 8)) for k in range(1, 8)]
    up_2, down_2 = at(lax.rem(row + 8, 32), col), at(lax.rem(row + 24, 32), col)
    core_row = row + 1 - 2 * co
    xl_row = row + 2 - 4 * xl
    other_col = col + 1 - 2 * xh
    loads = (
        pltpu.make_async_copy(acc_hbm, acc_ref, load_s.at[0]),
        pltpu.make_async_copy(band_hbm, band_ref, load_s.at[1]),
    )
    for load in loads:
        load.start()
    barrier = pltpu.get_barrier_semaphore()
    greet = [up, down, up_2, down_2] + col_peers + [at(core_row, col), at(xl_row, col), at(xl_row, other_col), at(core_row, other_col)]
    for peer in greet:
        pl.semaphore_signal(barrier, inc=1, device_id=peer, device_id_type=MESH)
    pl.semaphore_wait(barrier, len(greet))

    def cot_piece(row_):
        return cot_all.at[pl.ds(pl.multiple_of(16 * row_, 16), 16)]

    def act_piece(col_):
        return act_all.at[pl.ds(pl.multiple_of(64 * col_, 64), 64)]

    order = (1, 7, 2, 6, 3, 5, 4)
    start(cot_ref, cot_piece(row), cz_s.at[1], cz_r.at[1], up)
    start(cot_ref, cot_piece(row), cz_s.at[7], cz_r.at[7], down)
    start(cot_ref, cot_piece(row), cz_s.at[2], cz_r.at[2], up_2)
    start(cot_ref, cot_piece(row), cz_s.at[6], cz_r.at[6], down_2)
    start(cot_ref, cot_piece(row), cx_s.at[0], cx_r.at[0], at(xl_row, col))
    start(cot_ref, cot_piece(row), cc_s.at[0], cc_r.at[0], at(core_row, col))
    for k in range(1, 8):
        start(act_ref, act_piece(col), act_s.at[k], act_r.at[k], at(row, lax.rem(col + k, 8)))
    cot_piece(row)[...] = cot_ref[...]
    act_piece(col)[...] = act_ref[...]

    onward = {1: (3, up_2), 2: (4, up_2), 7: (5, down_2)}

    def beside(k):
        piece_in = cot_piece(lax.rem(xl_row - 4 * k + 32, 32))
        arrived(piece_in, cx_r.at[k])
        start(piece_in, piece_in, cc_s.at[8 + k], cc_r.at[8 + k], at(core_row, col))

    after = {1: (0,), 7: (), 2: (1,), 6: (7,), 3: (2,), 5: (6,), 4: (3, 5, 4)}
    for k in order:
        piece_in = cot_piece(lax.rem(row - 4 * k + 32, 32))
        arrived(piece_in, cz_r.at[k])
        if k in onward:
            start(piece_in, piece_in, cz_s.at[onward[k][0]], cz_r.at[onward[k][0]], onward[k][1])
        start(piece_in, piece_in, cx_s.at[k], cx_r.at[k], at(xl_row, col))
        start(piece_in, piece_in, cc_s.at[k], cc_r.at[k], at(core_row, col))
        for other in after[k]:
            beside(other)
    for m in range(1, 8):
        arrived(act_piece(lax.rem(col - m + 8, 8)), act_r.at[m])
    act_t[...] = act_all[...].T
    for k in (0,) + order:
        arrived(cot_piece(lax.rem(core_row - 4 * k + 32, 32)), cc_r.at[k])
    for k in (0,) + order:
        arrived(cot_piece(lax.rem(core_row + 2 - 4 * xl - 4 * k + 32, 32)), cc_r.at[8 + k])

    same = xh == co
    own = jnp.where(same, A0, STAGE)
    size = 256 // CHUNKS

    def chunk(slot, i):
        if slot in (XP, XM):
            half_of, first = divmod(size * i, 128)
            return pan.at[XP + half_of, pl.ds(first + 128 * (slot - XP), size)]
        return pan.at[slot, pl.ds(size * i, size)]

    def swap(i):
        return send(chunk(STAGE, i), chunk(A0, i), sw_s.at[i], sw_r.at[i], at(4 * z + 2 * xl + xh, 2 * y + co))

    def go_up(i, source, to):
        return send(chunk(source, i), chunk(to, i), pan_s.at[to, i], pan_r.at[to, i], up)

    def go_down(i, source, to):
        return send(chunk(source, i), chunk(to, i), pan_s.at[to, i], pan_r.at[to, i], down)

    def own_over_z(i):
        if i < LEAD:
            go_up(i, A0, AM1).start()
        go_down(i, A0, AP1).start()

    loads[0].wait()
    tall = 128
    per = CHUNKS * tall // 256
    for j in range(256 // tall):
        rows = pl.ds(tall * j, tall)

        for n in range(7):
            columns = pl.ds(256 * n, 256)
            product = jnp.dot(act_t[rows, :], cot_all[:, columns], preferred_element_type=jnp.float32)
            pan[own, rows, columns] = (product + acc_ref[rows, columns].astype(jnp.float32)).astype(jnp.bfloat16)

        @pl.when(jnp.logical_not(same))
        def _():
            for i in range(per * j, per * (j + 1)):
                swap(i).start()

        @pl.when(same)
        def _():
            for i in range(per * j, per * (j + 1)):
                own_over_z(i)

    @pl.when(jnp.logical_not(same))
    def _():
        for i in range(CHUNKS):
            arrived(chunk(A0, i), sw_r.at[i])
            own_over_z(i)

    for i in range(CHUNKS):
        sent.extend((go_up(i, A0, AM1), go_down(i, A0, AP1)))

    firsts = [AP2 if a is None else a for a, _ in TASKS]
    seconds = [b for _, b in TASKS]

    def rank_of(dz, dx):
        zz, xx = lax.rem(z + dz + 8, 8), lax.rem(x + dx + 4, 4)
        return 4 * zz + 2 * lax.rem(xx, 2) + xx // 2

    ranks = [rank_of(*place) for place in PLACE]

    def either(t):
        return xh == 1 if t == 16 else xl == 1

    def block_of(t):
        first, second = TASKS[t]
        left = ranks[AP2] if first is None else ranks[first]
        right = ranks[second]
        if first is None:
            left = jnp.where(either(t), ranks[AM2], left)
        if t == 13:
            left, right = jnp.where(xl == 1, right, left), jnp.where(xl == 1, left, right)
        ahead = lax.rem(left - right + 32, 32)
        to_col = (ahead - 1) // 2
        return left, to_col, lax.rem(ahead + 1, 2)

    blocks = [None] + [block_of(t) for t in range(1, N)]

    def task(t):
        other = ((t >= 13) & (t <= 15)) & (xl == 1) | (t == 16) & (xh == 1)
        left = jnp.where(other, AM2, pick(t, firsts))
        return left, jnp.where((t == 13) & (xl == 1), AP2, pick(t, seconds))

    def span(u):
        t, n, g = UNITS[u]
        return pl.ds(t, n), pl.ds(0, GROUPS) if g is None else pl.ds(g, 1)

    def core_copy(u):
        tasks, groups = span(u)
        return send(
            prod.at[tasks, groups, pl.ds(pl.multiple_of(128 * (1 - co), 128), 128)], core_in.at[tasks, groups],
            core_s.at[u], core_r.at[u], at(core_row, col),
        )

    def multiply(left, right):
        return lax.dot_general(
            pan[left], right, (((1,), (1,)), ((), ())), preferred_element_type=jnp.float32
        )

    def compute(u):
        first_task, count, g = UNITS[u]
        if g is None:

            @pl.loop(first_task, first_task + count)
            def _(t):
                left, right = task(t)
                block = multiply(left, pan[right])
                prod[t, 0] = block[:, :128]
                prod[t, 1] = block[:, 128:]

        else:
            t, last = first_task, first_task + count
            while t < last:
                if TASKS[t][1] == XP:
                    pairs = 1
                    while t + 2 * pairs + 1 < last and TASKS[t + 2 * pairs][1] == XP:
                        pairs += 1

                    @pl.loop(0, pairs)
                    def _(n, t=t):
                        left, _ = task(t + 2 * n)
                        block = multiply(left, pan[XP + g])
                        prod[t + 2 * n, g] = block[:, :128]
                        prod[t + 2 * n + 1, g] = block[:, 128:]

                    t += 2 * pairs
                else:
                    others = 1
                    while t + others < last and TASKS[t + others][1] != XP:
                        others += 1

                    @pl.loop(t, t + others)
                    def _(n):
                        left, right = task(n)
                        prod[n, g] = multiply(left, pan[right, pl.ds(128 * g, 128)])

                    t += others
        start_again(core_copy(u))

    def start_again(copy):
        copy.start()
        sent.append(copy)

    def add_cores(u):
        tasks, groups = span(u)
        arrived(core_in.at[tasks, groups], core_r.at[u])
        half[tasks, groups] = prod[tasks, groups, pl.ds(pl.multiple_of(128 * co, 128), 128)] + core_in[tasks, groups]
        for k in (2, 1, 3):
            to = lax.rem(y + k, 4)
            start_again(send(
                half.at[tasks, groups, pl.ds(pl.multiple_of(32 * to, 32), 32)], y_in.at[k - 1, tasks, groups],
                y_s.at[u, k - 1], y_r.at[u, k - 1], dev(0, 0, k, co),
            ))

    part = 4 * co + y
    rows_of_part = pl.ds(pl.multiple_of(32 * part, 32), 32)

    def deliver(src, dst, s_sem, r_sem, to_row, to_col, begin):
        here = (to_row == row) & (to_col == col)
        if begin:

            @pl.when(here)
            def _():
                pltpu.make_async_copy(src, dst, r_sem).start()

        @pl.when(jnp.logical_not(here))
        def _():
            copy = send(src, dst, s_sem, r_sem, at(to_row, to_col))
            if begin:
                copy.start()
            else:
                copy.wait_send()

    def deliver_diagonal(begin):
        deliver(piece.at[0], fin_diag, find_s.at[0], find_r.at[0], ranks[A0], part, begin)

    def deliver_block(t, g, begin):
        to_row, to_col, slot = blocks[t]
        deliver(
            piece.at[t, g], fin.at[slot, g, rows_of_part], fin_s.at[t, g], fin_r.at[slot, g, part],
            to_row, to_col, begin,
        )

    def add_y(u):
        tasks, groups = span(u)
        for k in range(3):
            arrived(y_in.at[k, tasks, groups], y_r.at[u, k])
        mine = half[tasks, groups, pl.ds(pl.multiple_of(32 * y, 32), 32)]
        piece[tasks, groups] = (mine + y_in[1, tasks, groups]) + (y_in[0, tasks, groups] + y_in[2, tasks, groups])

    def finish(u):
        first_task, count, group = UNITS[u]

        for t in range(first_task, first_task + count):
            for g in range(GROUPS):
                if group is None or group == g:
                    deliver_block(t, g, True)

    def last_panel(i):
        for slot in (XP, XM):
            arrived(chunk(slot, i), pan_r.at[slot, i])
        source, device = (XM, dev(0, 1, 0, co)) if i % 2 else (XP, dev(0, -1, 0, co))
        start(chunk(source, i), chunk(XX, i), pan_s.at[XX, i], pan_r.at[XX, i], device)

    def last_arrived(i):
        arrived(chunk(XX, i), pan_r.at[XX, i])

    def arm(k):
        arrived(chunk(AM2, k), pan_r.at[AM2, k])
        start(chunk(AM2, k), chunk(XP, k), pan_s.at[XP, k], pan_r.at[XP, k], dev(0, -1, 0, co))
        start(chunk(AM2, k), chunk(XM, k), pan_s.at[XM, k], pan_r.at[XM, k], dev(0, 1, 0, co))
        if k >= 1:
            last_panel(k - 1)

    compute(0)
    for i in range(CHUNKS):
        if i >= LEAD:
            arm(i - LEAD)
        arrived(chunk(AM1, i), pan_r.at[AM1, i])
        start_again(go_up(i, AM1, AM2))
        if i + LEAD < CHUNKS:
            go_up(i + LEAD, A0, AM1).start()
        arrived(chunk(AP1, i), pan_r.at[AP1, i])
        start_again(go_down(i, AP1, AP2))
        if i == 1:
            add_cores(0)
        if i == 4:
            add_y(0)
            deliver_diagonal(True)
    for k in range(CHUNKS - LEAD, CHUNKS):
        arm(k)
        if k == 4:
            compute(1)
            compute(2)
        if k == 5:
            compute(11)
            add_cores(1)
            add_cores(2)
        if k == 6:
            add_cores(11)
            for i in range(4):
                last_arrived(i)
            compute(4)
        if k == 7:
            add_cores(4)
            add_y(1)
            finish(1)
    compute(3)
    for i in range(CHUNKS):
        arrived(chunk(AP2, i), pan_r.at[AP2, i])
    compute(6)
    compute(10)
    last_panel(CHUNKS - 1)
    add_cores(3)
    add_cores(6)
    compute(8)
    add_cores(10)
    compute(9)
    add_cores(8)
    add_cores(9)
    for u in (2, 11, 4, 3, 6):
        add_y(u)
        finish(u)
    for i in range(4, CHUNKS):
        last_arrived(i)
    compute(5)
    compute(7)
    add_y(10)
    finish(10)
    add_cores(5)
    add_cores(7)
    for u in (8, 9, 5, 7):
        add_y(u)
        finish(u)

    loads[1].wait()
    arrived(fin_diag, find_r.at[0])
    for g in range(GROUPS):
        lanes = pl.ds(128 * g, 128)
        diag_out[:, lanes] = DECAY * diag_ref[:, lanes] + (1.0 - DECAY) * fin_diag[g]
    for slot in range(2):
        for k in range(8):
            for g in range(GROUPS):
                arrived(fin.at[slot, g, pl.ds(32 * k, 32)], fin_r.at[slot, g, k])
        for g in range(GROUPS):
            lanes = pl.ds(128 * g, 128)
            band_out[:, slot, lanes] = DECAY * band_ref[:, slot, lanes] + (1.0 - DECAY) * fin[slot, g]

    for copy in sent:
        copy.wait_send()

    @pl.when(jnp.logical_not(same))
    def _():
        for i in range(CHUNKS):
            swap(i).wait_send()

    deliver_diagonal(False)

    for t in range(1, N):
        for g in range(GROUPS):
            deliver_block(t, g, False)


def body(activations, cotangent, accumulated, band_old, diagonal_old):
    dma = pltpu.SemaphoreType.DMA
    f32, bf16 = jnp.float32, jnp.bfloat16
    vmem = pl.BlockSpec(memory_space=pltpu.VMEM)
    hbm = pl.BlockSpec(memory_space=pl.ANY)
    return pl.pallas_call(
        kernel,
        out_shape=(
            jax.ShapeDtypeStruct(band_old.shape, f32),
            jax.ShapeDtypeStruct(diagonal_old.shape, f32),
        ),
        in_specs=[vmem, vmem, hbm, hbm, vmem],
        out_specs=(vmem, vmem),
        scratch_shapes=[
            pltpu.VMEM(accumulated.shape, bf16),
            pltpu.VMEM(band_old.shape, f32),
            dma((2,)),
            pltpu.VMEM((512, 256), bf16),
            pltpu.VMEM((256, 512), bf16),
            pltpu.VMEM((512, 1792), bf16),
            pltpu.VMEM((9, 256, 1792), bf16),
            pltpu.VMEM((N, GROUPS, 256, 128), f32),
            pltpu.VMEM((N, GROUPS, 128, 128), f32),
            pltpu.VMEM((N, GROUPS, 128, 128), f32),
            pltpu.VMEM((3, N, GROUPS, 32, 128), f32),
            pltpu.VMEM((N, GROUPS, 32, 128), f32),
            pltpu.VMEM((2, GROUPS, 256, 128), f32),
            pltpu.VMEM((GROUPS, 32, 128), f32),
            dma((8,)), dma((8,)), dma((8,)), dma((8,)), dma((8,)), dma((8,)), dma((16,)), dma((16,)),
            dma((CHUNKS,)), dma((CHUNKS,)), dma((8, CHUNKS)), dma((8, CHUNKS)),
            dma((len(UNITS),)), dma((len(UNITS),)), dma((len(UNITS), 3)), dma((len(UNITS), 3)),
            dma((N, GROUPS)), dma((2, GROUPS, 8)), dma((1,)), dma((1,)),
        ],
        compiler_params=pltpu.CompilerParams(
            collective_id=0, has_side_effects=True, vmem_limit_bytes=56 * 2**20
        ),
    )(activations, cotangent, accumulated, band_old, diagonal_old)


def solution(mesh):
    in_specs = (
        P("col", "row"),
        P("row", "col"),
        P("row", "col"),
        P("row", "col", None),
        P(("row", "col"), None),
    )
    out_specs = (P("row", "col", None), P(("row", "col"), None))
    return jax.shard_map(body, mesh=mesh, in_specs=in_specs, out_specs=out_specs, check_vma=False)
```

```python
import jax
import jax.numpy as jnp
from jax import lax
from jax.experimental import pallas as pl
from jax.experimental.pallas import tpu as pltpu
from jax.sharding import PartitionSpec as P

MESH = pl.DeviceIdType.MESH
DECAY = 0.95
CHUNKS = 8
GROUPS = 2
LEAD = 4

A0, AM1, AP1, AM2, AP2, XP, XM, XX, STAGE = range(9)
PLACE = ((0, 0), (-1, 0), (1, 0), (-2, 0), (2, 0), (-2, 1), (-2, -1), (-2, 2))
TASKS = (
    (A0, A0), (A0, AM1), (AP1, AM1),
    (AP1, AM2), (AP1, XP), (AP1, XM), (A0, XP), (A0, XM), (AM1, XP), (AM1, XM),
    (AP1, XX), (A0, XX), (AM1, XX),
    (AP2, AM2), (None, XP), (None, XM), (None, XX),
)
N = len(TASKS)
UNITS = (
    (0, 1, None), (1, 2, None),
    (3, 3, 0), (3, 1, 1), (10, 3, 0), (10, 3, 1),
    (13, 1, None), (16, 1, 1), (4, 6, 1), (14, 2, 1), (14, 3, 0), (6, 4, 0),
)


def pick(index, values):
    result = jnp.int32(values[0])
    for i, value in enumerate(values):
        if i and value != values[0]:
            result = jnp.where(index == i, jnp.int32(value), result)
    return result


def kernel(
    act_ref, cot_ref, acc_hbm, band_hbm, diag_ref, band_out, diag_out,
    acc_ref, band_ref, load_s,
    act_all, act_t, cot_all, pan, prod, core_in, half, y_in, piece, fin, fin_diag,
    act_s, act_r, cz_s, cz_r, cx_s, cx_r, cc_s, cc_r, sw_s, sw_r, pan_s, pan_r,
    core_s, core_r, y_s, y_r, fin_s, fin_r, find_s, find_r,
):
    row = lax.axis_index("row")
    col = lax.axis_index("col")
    z, xl, co = row // 4, lax.rem(row // 2, 2), lax.rem(row, 2)
    y, xh = col // 2, lax.rem(col, 2)
    x = 2 * xh + xl

    def at(row_, col_):
        return {"row": row_, "col": col_}

    def dev(dz, dx, dy, core):
        zz, xx, yy = lax.rem(z + dz + 8, 8), lax.rem(x + dx + 4, 4), lax.rem(y + dy + 4, 4)
        return at(4 * zz + 2 * lax.rem(xx, 2) + core, 2 * yy + xx // 2)

    def send(src, dst, s_sem, r_sem, device):
        return pltpu.make_async_remote_copy(
            src_ref=src, dst_ref=dst, send_sem=s_sem, recv_sem=r_sem, device_id=device, device_id_type=MESH
        )

    def arrived(dst, sem):
        pltpu.make_async_copy(dst, dst, sem).wait()

    sent = []

    def start(*args):
        copy = send(*args)
        copy.start()
        sent.append(copy)

    up, down = at(lax.rem(row + 4, 32), col), at(lax.rem(row + 28, 32), col)
    col_peers = [at(row, lax.rem(col + k, 8)) for k in range(1, 8)]
    up_2, down_2 = at(lax.rem(row + 8, 32), col), at(lax.rem(row + 24, 32), col)
    core_row = row + 1 - 2 * co
    xl_row = row + 2 - 4 * xl
    other_col = col + 1 - 2 * xh
    loads = (
        pltpu.make_async_copy(acc_hbm, acc_ref, load_s.at[0]),
        pltpu.make_async_copy(band_hbm, band_ref, load_s.at[1]),
    )
    for load in loads:
        load.start()
    barrier = pltpu.get_barrier_semaphore()
    greet = [up, down, up_2, down_2] + col_peers + [at(core_row, col), at(xl_row, col), at(xl_row, other_col), at(core_row, other_col)]
    for peer in greet:
        pl.semaphore_signal(barrier, inc=1, device_id=peer, device_id_type=MESH)
    pl.semaphore_wait(barrier, len(greet))

    def cot_piece(row_):
        return cot_all.at[pl.ds(pl.multiple_of(16 * row_, 16), 16)]

    def act_piece(col_):
        return act_all.at[pl.ds(pl.multiple_of(64 * col_, 64), 64)]

    order = (1, 7, 2, 6, 3, 5, 4)
    start(cot_ref, cot_piece(row), cz_s.at[1], cz_r.at[1], up)
    start(cot_ref, cot_piece(row), cz_s.at[7], cz_r.at[7], down)
    start(cot_ref, cot_piece(row), cz_s.at[2], cz_r.at[2], up_2)
    start(cot_ref, cot_piece(row), cz_s.at[6], cz_r.at[6], down_2)
    start(cot_ref, cot_piece(row), cx_s.at[0], cx_r.at[0], at(xl_row, col))
    start(cot_ref, cot_piece(row), cc_s.at[0], cc_r.at[0], at(core_row, col))
    for k in range(1, 8):
        start(act_ref, act_piece(col), act_s.at[k], act_r.at[k], at(row, lax.rem(col + k, 8)))
    cot_piece(row)[...] = cot_ref[...]
    act_piece(col)[...] = act_ref[...]

    onward = {1: (3, up_2), 2: (4, up_2), 7: (5, down_2)}

    def beside(k):
        piece_in = cot_piece(lax.rem(xl_row - 4 * k + 32, 32))
        arrived(piece_in, cx_r.at[k])
        start(piece_in, piece_in, cc_s.at[8 + k], cc_r.at[8 + k], at(core_row, col))

    after = {1: (0,), 7: (), 2: (1,), 6: (7,), 3: (2,), 5: (6,), 4: (3, 5, 4)}
    for k in order:
        piece_in = cot_piece(lax.rem(row - 4 * k + 32, 32))
        arrived(piece_in, cz_r.at[k])
        if k in onward:
            start(piece_in, piece_in, cz_s.at[onward[k][0]], cz_r.at[onward[k][0]], onward[k][1])
        start(piece_in, piece_in, cx_s.at[k], cx_r.at[k], at(xl_row, col))
        start(piece_in, piece_in, cc_s.at[k], cc_r.at[k], at(core_row, col))
        for other in after[k]:
            beside(other)
    for m in range(1, 8):
        arrived(act_piece(lax.rem(col - m + 8, 8)), act_r.at[m])
    act_t[...] = act_all[...].T
    for k in (0,) + order:
        arrived(cot_piece(lax.rem(core_row - 4 * k + 32, 32)), cc_r.at[k])
    for k in (0,) + order:
        arrived(cot_piece(lax.rem(core_row + 2 - 4 * xl - 4 * k + 32, 32)), cc_r.at[8 + k])

    same = xh == co
    own = jnp.where(same, A0, STAGE)
    size = 256 // CHUNKS

    def chunk(slot, i):
        if slot in (XP, XM):
            half_of, first = divmod(size * i, 128)
            return pan.at[XP + half_of, pl.ds(first + 128 * (slot - XP), size)]
        return pan.at[slot, pl.ds(size * i, size)]

    def swap(i):
        return send(chunk(STAGE, i), chunk(A0, i), sw_s.at[i], sw_r.at[i], at(4 * z + 2 * xl + xh, 2 * y + co))

    def go_up(i, source, to):
        return send(chunk(source, i), chunk(to, i), pan_s.at[to, i], pan_r.at[to, i], up)

    def go_down(i, source, to):
        return send(chunk(source, i), chunk(to, i), pan_s.at[to, i], pan_r.at[to, i], down)

    def own_over_z(i):
        if i < LEAD:
            go_up(i, A0, AM1).start()
        go_down(i, A0, AP1).start()

    loads[0].wait()
    tall = 128
    per = CHUNKS * tall // 256
    for j in range(256 // tall):
        rows = pl.ds(tall * j, tall)

        for n in range(7):
            columns = pl.ds(256 * n, 256)
            product = jnp.dot(act_t[rows, :], cot_all[:, columns], preferred_element_type=jnp.float32)
            pan[own, rows, columns] = (product + acc_ref[rows, columns].astype(jnp.float32)).astype(jnp.bfloat16)

        @pl.when(jnp.logical_not(same))
        def _():
            for i in range(per * j, per * (j + 1)):
                swap(i).start()

        @pl.when(same)
        def _():
            for i in range(per * j, per * (j + 1)):
                own_over_z(i)

    @pl.when(jnp.logical_not(same))
    def _():
        for i in range(CHUNKS):
            arrived(chunk(A0, i), sw_r.at[i])
            own_over_z(i)

    for i in range(CHUNKS):
        sent.extend((go_up(i, A0, AM1), go_down(i, A0, AP1)))

    firsts = [AP2 if a is None else a for a, _ in TASKS]
    seconds = [b for _, b in TASKS]

    def rank_of(dz, dx):
        zz, xx = lax.rem(z + dz + 8, 8), lax.rem(x + dx + 4, 4)
        return 4 * zz + 2 * lax.rem(xx, 2) + xx // 2

    ranks = [rank_of(*place) for place in PLACE]

    def either(t):
        return xh == 1 if t == 16 else xl == 1

    def block_of(t):
        first, second = TASKS[t]
        left = ranks[AP2] if first is None else ranks[first]
        right = ranks[second]
        if first is None:
            left = jnp.where(either(t), ranks[AM2], left)
        if t == 13:
            left, right = jnp.where(xl == 1, right, left), jnp.where(xl == 1, left, right)
        ahead = lax.rem(left - right + 32, 32)
        to_col = (ahead - 1) // 2
        return left, to_col, lax.rem(ahead + 1, 2)

    blocks = [None] + [block_of(t) for t in range(1, N)]

    def task(t):
        other = ((t >= 13) & (t <= 15)) & (xl == 1) | (t == 16) & (xh == 1)
        left = jnp.where(other, AM2, pick(t, firsts))
        return left, jnp.where((t == 13) & (xl == 1), AP2, pick(t, seconds))

    def span(u):
        t, n, g = UNITS[u]
        return pl.ds(t, n), pl.ds(0, GROUPS) if g is None else pl.ds(g, 1)

    def core_copy(u):
        tasks, groups = span(u)
        return send(
            prod.at[tasks, groups, pl.ds(pl.multiple_of(128 * (1 - co), 128), 128)], core_in.at[tasks, groups],
            core_s.at[u], core_r.at[u], at(core_row, col),
        )

    def multiply(left, right):
        return lax.dot_general(
            pan[left], right, (((1,), (1,)), ((), ())), preferred_element_type=jnp.float32
        )

    def compute(u):
        first_task, count, g = UNITS[u]
        if g is None:

            @pl.loop(first_task, first_task + count)
            def _(t):
                left, right = task(t)
                block = multiply(left, pan[right])
                prod[t, 0] = block[:, :128]
                prod[t, 1] = block[:, 128:]

        else:
            t, last = first_task, first_task + count
            while t < last:
                if TASKS[t][1] == XP:
                    pairs = 1
                    while t + 2 * pairs + 1 < last and TASKS[t + 2 * pairs][1] == XP:
                        pairs += 1

                    @pl.loop(0, pairs)
                    def _(n, t=t):
                        left, _ = task(t + 2 * n)
                        block = multiply(left, pan[XP + g])
                        prod[t + 2 * n, g] = block[:, :128]
                        prod[t + 2 * n + 1, g] = block[:, 128:]

                    t += 2 * pairs
                else:
                    others = 1
                    while t + others < last and TASKS[t + others][1] != XP:
                        others += 1

                    @pl.loop(t, t + others)
                    def _(n):
                        left, right = task(n)
                        prod[n, g] = multiply(left, pan[right, pl.ds(128 * g, 128)])

                    t += others
        start_again(core_copy(u))

    def start_again(copy):
        copy.start()
        sent.append(copy)

    def add_cores(u):
        tasks, groups = span(u)
        arrived(core_in.at[tasks, groups], core_r.at[u])
        half[tasks, groups] = prod[tasks, groups, pl.ds(pl.multiple_of(128 * co, 128), 128)] + core_in[tasks, groups]
        for k in (2, 1, 3):
            to = lax.rem(y + k, 4)
            start_again(send(
                half.at[tasks, groups, pl.ds(pl.multiple_of(32 * to, 32), 32)], y_in.at[k - 1, tasks, groups],
                y_s.at[u, k - 1], y_r.at[u, k - 1], dev(0, 0, k, co),
            ))

    part = 4 * co + y
    rows_of_part = pl.ds(pl.multiple_of(32 * part, 32), 32)

    def deliver(src, dst, s_sem, r_sem, to_row, to_col, begin):
        here = (to_row == row) & (to_col == col)
        if begin:

            @pl.when(here)
            def _():
                pltpu.make_async_copy(src, dst, r_sem).start()

        @pl.when(jnp.logical_not(here))
        def _():
            copy = send(src, dst, s_sem, r_sem, at(to_row, to_col))
            if begin:
                copy.start()
            else:
                copy.wait_send()

    def deliver_diagonal(begin):
        deliver(piece.at[0], fin_diag, find_s.at[0], find_r.at[0], ranks[A0], part, begin)

    def deliver_block(t, g, begin):
        to_row, to_col, slot = blocks[t]
        deliver(
            piece.at[t, g], fin.at[slot, g, rows_of_part], fin_s.at[t, g], fin_r.at[slot, g, part],
            to_row, to_col, begin,
        )

    def add_y(u):
        tasks, groups = span(u)
        for k in range(3):
            arrived(y_in.at[k, tasks, groups], y_r.at[u, k])
        mine = half[tasks, groups, pl.ds(pl.multiple_of(32 * y, 32), 32)]
        piece[tasks, groups] = (mine + y_in[1, tasks, groups]) + (y_in[0, tasks, groups] + y_in[2, tasks, groups])

    def finish(u):
        first_task, count, group = UNITS[u]

        for t in range(first_task, first_task + count):
            for g in range(GROUPS):
                if group is None or group == g:
                    deliver_block(t, g, True)

    def last_panel(i):
        for slot in (XP, XM):
            arrived(chunk(slot, i), pan_r.at[slot, i])
        source, device = (XM, dev(0, 1, 0, co)) if i % 2 else (XP, dev(0, -1, 0, co))
        start(chunk(source, i), chunk(XX, i), pan_s.at[XX, i], pan_r.at[XX, i], device)

    def last_arrived(i):
        arrived(chunk(XX, i), pan_r.at[XX, i])

    def arm(k):
        arrived(chunk(AM2, k), pan_r.at[AM2, k])
        start(chunk(AM2, k), chunk(XP, k), pan_s.at[XP, k], pan_r.at[XP, k], dev(0, -1, 0, co))
        start(chunk(AM2, k), chunk(XM, k), pan_s.at[XM, k], pan_r.at[XM, k], dev(0, 1, 0, co))
        if k >= 1:
            last_panel(k - 1)

    compute(0)
    for i in range(CHUNKS):
        if i >= LEAD:
            arm(i - LEAD)
        arrived(chunk(AM1, i), pan_r.at[AM1, i])
        start_again(go_up(i, AM1, AM2))
        if i + LEAD < CHUNKS:
            go_up(i + LEAD, A0, AM1).start()
        arrived(chunk(AP1, i), pan_r.at[AP1, i])
        start_again(go_down(i, AP1, AP2))
        if i == 1:
            add_cores(0)
        if i == 4:
            add_y(0)
            deliver_diagonal(True)
    compute(1)
    for k in range(CHUNKS - LEAD, CHUNKS):
        arm(k)
        if k == 4:
            compute(2)
            add_cores(1)
        if k == 5:
            compute(11)
            add_cores(2)
        if k == 6:
            add_cores(11)
            for i in range(4):
                last_arrived(i)
            compute(4)
            add_y(1)
            finish(1)
        if k == 7:
            add_cores(4)
    compute(3)
    for i in range(CHUNKS):
        arrived(chunk(AP2, i), pan_r.at[AP2, i])
    compute(6)
    compute(10)
    last_panel(CHUNKS - 1)
    add_cores(3)
    add_cores(6)
    compute(8)
    add_cores(10)
    compute(9)
    add_cores(8)
    add_cores(9)
    for u in (2, 11, 4, 3, 6):
        add_y(u)
        finish(u)
    for i in range(4, CHUNKS):
        last_arrived(i)
    compute(5)
    compute(7)
    add_cores(5)
    add_cores(7)
    for u in (10, 8, 9, 5, 7):
        add_y(u)
        finish(u)

    loads[1].wait()
    arrived(fin_diag, find_r.at[0])
    for g in range(GROUPS):
        lanes = pl.ds(128 * g, 128)
        diag_out[:, lanes] = DECAY * diag_ref[:, lanes] + (1.0 - DECAY) * fin_diag[g]
    for slot in range(2):
        for k in range(8):
            for g in range(GROUPS):
                arrived(fin.at[slot, g, pl.ds(32 * k, 32)], fin_r.at[slot, g, k])
        for g in range(GROUPS):
            lanes = pl.ds(128 * g, 128)
            band_out[:, slot, lanes] = DECAY * band_ref[:, slot, lanes] + (1.0 - DECAY) * fin[slot, g]

    for copy in sent:
        copy.wait_send()

    @pl.when(jnp.logical_not(same))
    def _():
        for i in range(CHUNKS):
            swap(i).wait_send()

    deliver_diagonal(False)

    for t in range(1, N):
        for g in range(GROUPS):
            deliver_block(t, g, False)


def body(activations, cotangent, accumulated, band_old, diagonal_old):
    dma = pltpu.SemaphoreType.DMA
    f32, bf16 = jnp.float32, jnp.bfloat16
    vmem = pl.BlockSpec(memory_space=pltpu.VMEM)
    hbm = pl.BlockSpec(memory_space=pl.ANY)
    return pl.pallas_call(
        kernel,
        out_shape=(
            jax.ShapeDtypeStruct(band_old.shape, f32),
            jax.ShapeDtypeStruct(diagonal_old.shape, f32),
        ),
        in_specs=[vmem, vmem, hbm, hbm, vmem],
        out_specs=(vmem, vmem),
        scratch_shapes=[
            pltpu.VMEM(accumulated.shape, bf16),
            pltpu.VMEM(band_old.shape, f32),
            dma((2,)),
            pltpu.VMEM((512, 256), bf16),
            pltpu.VMEM((256, 512), bf16),
            pltpu.VMEM((512, 1792), bf16),
            pltpu.VMEM((9, 256, 1792), bf16),
            pltpu.VMEM((N, GROUPS, 256, 128), f32),
            pltpu.VMEM((N, GROUPS, 128, 128), f32),
            pltpu.VMEM((N, GROUPS, 128, 128), f32),
            pltpu.VMEM((3, N, GROUPS, 32, 128), f32),
            pltpu.VMEM((N, GROUPS, 32, 128), f32),
            pltpu.VMEM((2, GROUPS, 256, 128), f32),
            pltpu.VMEM((GROUPS, 32, 128), f32),
            dma((8,)), dma((8,)), dma((8,)), dma((8,)), dma((8,)), dma((8,)), dma((16,)), dma((16,)),
            dma((CHUNKS,)), dma((CHUNKS,)), dma((8, CHUNKS)), dma((8, CHUNKS)),
            dma((len(UNITS),)), dma((len(UNITS),)), dma((len(UNITS), 3)), dma((len(UNITS), 3)),
            dma((N, GROUPS)), dma((2, GROUPS, 8)), dma((1,)), dma((1,)),
        ],
        compiler_params=pltpu.CompilerParams(
            collective_id=0, has_side_effects=True, vmem_limit_bytes=56 * 2**20
        ),
    )(activations, cotangent, accumulated, band_old, diagonal_old)


def solution(mesh):
    in_specs = (
        P("col", "row"),
        P("row", "col"),
        P("row", "col"),
        P("row", "col", None),
        P(("row", "col"), None),
    )
    out_specs = (P("row", "col", None), P(("row", "col"), None))
    return jax.shard_map(body, mesh=mesh, in_specs=in_specs, out_specs=out_specs, check_vma=False)
```
